128 devices in a mesh: outer: 8 (over y, core), inner: 16 (over z, x).
Axes of the slice: x: 4, y: 4, z: 4, core: 2. Of those that a mesh axis runs over, the one named last changes fastest.
Arguments:
- layer_input: bfloat16 [16384, 7168], P(('outer', 'inner')), may hold values from -6 to 6
- out_grad: bfloat16 [16384, 7168], P(('outer', 'inner')), may hold values from -3 to 3
- expert_ids: int32 [16384, 8], P(('outer', 'inner')), may hold values from 0 to 255, as said below
- route_scales: float32 [16384, 8], P(('outer', 'inner')), may hold values from 0.25 to 2.5
- w_gate: bfloat16 [8, 7168, 2048], P('outer', None, 'inner'), may hold values from -0.0625 to 0.0625
- w_up: bfloat16 [8, 7168, 2048], P('outer', None, 'inner'), may hold values from -0.0625 to 0.0625
- w_down: bfloat16 [8, 2048, 7168], P('outer', 'inner'), may hold values from -0.125 to 0.125
Outputs:
- in_grad: bfloat16 [16384, 7168], P(('outer', 'inner'))
- grad_w_gate: float32 [8, 7168, 2048], P('outer', None, 'inner')
- grad_w_up: float32 [8, 7168, 2048], P('outer', None, 'inner')
- grad_w_down: float32 [8, 2048, 7168], P('outer', 'inner')
The draws below stay inside these ranges and needn't reach their ends.
Inputs may be any that keep to these rules, and one draw needn't show every extreme that they name: `expert_ids`: each row names 8 different experts. In each device's aligned block of 128 rows at most 6 rows name any one expert below 8, and in every draw one expert below 8 is named by exactly 6 rows of every block.
All inputs are finite; a program needn't handle non-finite values.
Results may differ from the reference program's by a relative error of at most 0.014.
Values may be sent and summed in bfloat16 or wider, within the bound.
A program may use at most 192 MiB of HBM per device.

```python
import math
import jax
import jax.numpy as jnp
from jax import lax

D = 7168
F = 2048
EXPERTS = 256
TOPK = 8
TOK_DEV = 128
CAP = 6
FLIGHT = 8
HID = 128
TOKENS = 16384
N_INNER = 16


def draw_expert_ids(key, part):
    block_count = TOKENS // TOK_DEV
    keys = jax.random.split(key, 5)
    order = jax.random.permutation(keys[0], FLIGHT)
    hot_first = order[0]
    hot_second = order[1]
    expert_row = jnp.arange(FLIGHT, dtype=jnp.int32)
    upper = jnp.where(expert_row == hot_second, CAP, CAP // 3)
    counts = jax.random.randint(keys[1], (block_count, FLIGHT), 0, upper[None, :] + 1)
    counts = jnp.where(expert_row[None, :] == hot_first, CAP, counts)
    perm_keys = jax.random.split(keys[2], block_count * FLIGHT)
    perms = jax.vmap(lambda single: jax.random.permutation(single, TOK_DEV))(perm_keys)
    ranks = jnp.argsort(perms, axis=1).reshape(block_count, FLIGHT, TOK_DEV)
    flags = (ranks < counts[:, :, None]).astype(jnp.int32)
    flags = jnp.transpose(flags, (0, 2, 1)).reshape(TOKENS, FLIGHT)
    flags = jnp.concatenate([flags, jnp.zeros((TOKENS, TOPK - FLIGHT), jnp.int32)], axis=1)
    offset = jax.random.randint(keys[3], (TOKENS, 1), 0, EXPERTS - FLIGHT)
    slot_row = jnp.arange(TOPK, dtype=jnp.int32)[None, :]
    outside = FLIGHT + (offset + slot_row) % (EXPERTS - FLIGHT)
    chosen = jnp.where(flags == 1, slot_row, outside)
    shuffle = jax.random.randint(keys[4], (TOKENS, TOPK), 0, 1 << 20) * TOPK + slot_row
    order_rows = jnp.argsort(shuffle, axis=1)
    return jnp.take_along_axis(chosen, order_rows, axis=1).astype(jnp.int32)


def shard_levels(stream_key, dims, pieces, least, largest):
    def one(dim, parts):
        draws = jax.random.uniform(jax.random.fold_in(jax.random.fold_in(stream_key, 6), dim), (parts,), jnp.float32, least / len(pieces), largest / len(pieces))
        return jnp.repeat(jnp.exp(draws), dims[dim] // parts).reshape((-1,) + (1,) * (len(dims) - dim - 1))

    gain = one(*pieces[0])
    for cut in pieces[1:]:
        gain = gain * one(*cut)
    return gain


def scatter_about(own_key, dims, spread, limit, shards=(), kind=jnp.bfloat16):
    values = jax.random.normal(own_key, dims, jnp.float32) * spread
    if len(shards) > 0:
        values = shard_levels(own_key, dims, shards, -0.22, 0.18) * values
    return jnp.clip(values, min=-limit, max=limit).astype(kind)


def setup_inputs(seed: int = 0) -> dict:
    seeds = jax.random.split(jax.random.key(seed), 8)
    return {
        "layer_input": scatter_about(seeds[0], (TOKENS, D), 1.0, 6.0, ((0, 128),)),
        "out_grad": scatter_about(seeds[1], (TOKENS, D), 0.5, 3.0, ((0, 128),)),
        "expert_ids": draw_expert_ids(jax.random.fold_in(seeds[7], 71), 0),
        "route_scales": jnp.clip(jnp.exp(math.log(2.5) - 2.3025851 * jax.random.uniform(seeds[3], (TOKENS, TOPK), jnp.float32) ** shard_levels(seeds[3], (TOKENS, TOPK), ((0, 128),), -0.2, 0.2)), 0.25, 2.5),
        "w_gate": scatter_about(seeds[4], (FLIGHT, D, F), D ** -0.5, 0.0625, ((0, 8), (2, 16))),
        "w_up": scatter_about(seeds[5], (FLIGHT, D, F), D ** -0.5, 0.0625, ((0, 8), (2, 16))),
        "w_down": scatter_about(seeds[6], (FLIGHT, F, D), F ** -0.5, 0.125, ((0, 8), (1, 16))),
    }


def expert_grads(layer_input, out_grad, table, scales, gate_w, up_w, down_w):
    rows_x = jnp.take(layer_input, table, axis=0, mode="fill", fill_value=0)
    rows_dy = jnp.take(out_grad, table, axis=0, mode="fill", fill_value=0)
    routed = (scales[:, None] * rows_dy.astype(jnp.float32)).astype(jnp.bfloat16)
    gate = jnp.dot(rows_x, gate_w, preferred_element_type=jnp.float32)
    up_val = jnp.dot(rows_x, up_w, preferred_element_type=jnp.float32)
    sigmoid_gate = jax.nn.sigmoid(gate)
    silu_gate = gate * sigmoid_gate
    act = (silu_gate * up_val).astype(jnp.bfloat16)
    hid_grad = lax.dot_general(routed, down_w, (((1,), (1,)), ((), ())), preferred_element_type=jnp.float32)
    gate_grad = (hid_grad * up_val * sigmoid_gate * (1.0 + gate * (1.0 - sigmoid_gate))).astype(jnp.bfloat16)
    up_grad = (hid_grad * silu_gate).astype(jnp.bfloat16)
    grad_down = lax.dot_general(act, routed, (((0,), (0,)), ((), ())), preferred_element_type=jnp.float32)
    grad_gate = lax.dot_general(rows_x, gate_grad, (((0,), (0,)), ((), ())), preferred_element_type=jnp.float32)
    grad_up = lax.dot_general(rows_x, up_grad, (((0,), (0,)), ((), ())), preferred_element_type=jnp.float32)

    def block_term(total, block):
        first = (block * HID).astype(jnp.int32)
        gate_cols = lax.dynamic_slice_in_dim(gate_grad, first, HID, 1)
        up_cols = lax.dynamic_slice_in_dim(up_grad, first, HID, 1)
        gate_part = lax.dynamic_slice_in_dim(gate_w, first, HID, 1)
        up_part = lax.dynamic_slice_in_dim(up_w, first, HID, 1)
        term = lax.dot_general(gate_cols, gate_part, (((1,), (1,)), ((), ())), preferred_element_type=jnp.float32)
        term = term + lax.dot_general(up_cols, up_part, (((1,), (1,)), ((), ())), preferred_element_type=jnp.float32)
        rounded = lax.optimization_barrier(term.astype(jnp.bfloat16))
        return total + rounded.astype(jnp.float32), None

    start_sum = jnp.zeros((rows_x.shape[0], D), jnp.float32)
    route_sum, unused = lax.scan(block_term, start_sum, jnp.arange(N_INNER, dtype=jnp.int32))
    return grad_gate, grad_up, grad_down, route_sum.astype(jnp.bfloat16)


def reference(layer_input, out_grad, expert_ids, route_scales, w_gate, w_up, w_down):
    block_count = TOKENS // TOK_DEV
    route_ids = expert_ids.reshape(block_count, TOK_DEV * TOPK).astype(jnp.int32)
    experts_row = jnp.arange(FLIGHT, dtype=jnp.int32)
    onehot = (route_ids[:, :, None] == experts_row[None, None, :]).astype(jnp.int32)
    position = jnp.sum((jnp.cumsum(onehot, axis=1) - onehot) * onehot, axis=2).astype(jnp.int32)
    block_index = jnp.arange(block_count, dtype=jnp.int32)[:, None]
    route_index = jnp.arange(TOK_DEV * TOPK, dtype=jnp.int32)[None, :]
    token_index = (block_index * TOK_DEV + route_index // TOPK).astype(jnp.int32)
    slot_total = FLIGHT * block_count * CAP
    valid = route_ids < FLIGHT
    slot = jnp.where(valid, (route_ids * block_count + block_index) * CAP + position, slot_total).astype(jnp.int32)
    table = jnp.full((slot_total + 1,), TOKENS, jnp.int32).at[slot.reshape(-1)].set(token_index.reshape(-1))
    scale_table = jnp.zeros((slot_total + 1,), jnp.float32).at[slot.reshape(-1)].set(route_scales.reshape(-1))
    table = table[:slot_total].reshape(FLIGHT, block_count * CAP)
    scale_table = scale_table[:slot_total].reshape(FLIGHT, block_count * CAP)

    def one_expert(items):
        return expert_grads(layer_input, out_grad, items[0], items[1], items[2], items[3], items[4])

    grad_gate, grad_up, grad_down, route_grad = lax.map(one_expert, (table, scale_table, w_gate, w_up, w_down))
    summed = jnp.zeros((TOKENS + 1, D), jnp.float32).at[table.reshape(-1)].add(route_grad.reshape(-1, D).astype(jnp.float32))
    in_grad = summed[:TOKENS].astype(jnp.bfloat16)
    return in_grad, grad_gate, grad_up, grad_down
```

```python
import jax
import jax.numpy as jnp
from jax import lax
from jax.experimental import pallas as pl
from jax.experimental.pallas import tpu as pltpu
from jax.sharding import PartitionSpec as P

CAP = 6
PAD = 8
SIDE = 4
BF = jnp.bfloat16
F32 = jnp.float32
MESH = pl.DeviceIdType.MESH
NN = (((1,), (0,)), ((), ()))
NT = (((1,), (1,)), ((), ()))
TN = (((0,), (0,)), ((), ()))


def dot(a, b, dims):
    return lax.dot_general(a, b, dims, preferred_element_type=F32)


def kernel(
    ids_ref, scale_ref, x_hbm, dy_hbm, wg_hbm, wu_hbm, wd_hbm,
    in_grad_hbm, gate_hbm, up_hbm, down_hbm,
    tok, wgu, wd, place, ysend, yrecv, back, rows, gu, hid, ggug, act,
    sf, rf, sn, rn, part, rf2, rn2, final, stage, stage_d,
    load_sem, y_send_sem, y_recv_sem, b_send_sem, b_recv_sem,
    ag_send, ag_recv, rs_send, rs_recv, out_sem, out_d_sem,
):
    n_out = ysend.shape[1]
    width = tok.shape[2]
    half = width // 2
    quarter = width // 4
    slots = n_out * CAP
    me_o = lax.axis_index("outer")
    me_i = lax.axis_index("inner")
    my_z = me_i // SIDE
    my_x = lax.rem(me_i, SIDE)

    def ring(v, k):
        return lax.rem(v + k, SIDE)

    def peer(d):
        return lax.rem(me_o + d, n_out)

    first = (my_x, my_z)
    second = (my_z, my_x)

    def block(a, f, s):
        return s * SIDE + f if a == 0 else f * SIDE + s

    barrier = pltpu.get_barrier_semaphore()
    plane = [
        my_z * SIDE + ring(my_x, 1), my_z * SIDE + ring(my_x, 3),
        ring(my_z, 1) * SIDE + my_x, ring(my_z, 3) * SIDE + my_x,
    ]
    for i in plane:
        pl.semaphore_signal(barrier, inc=1, device_id=(me_o, i), device_id_type=MESH)
    for d in range(1, n_out):
        pl.semaphore_signal(barrier, inc=1, device_id=(peer(d), me_i), device_id_type=MESH)

    loads = [
        pltpu.make_async_copy(x_hbm, tok.at[0], load_sem.at[0]),
        pltpu.make_async_copy(dy_hbm, tok.at[1], load_sem.at[1]),
        pltpu.make_async_copy(wg_hbm, wgu.at[:, pl.ds(0, 128)], load_sem.at[2]),
        pltpu.make_async_copy(wu_hbm, wgu.at[:, pl.ds(128, 128)], load_sem.at[3]),
        pltpu.make_async_copy(wd_hbm, wd, load_sem.at[4]),
    ]
    for c in loads:
        c.start()

    toks = ids_ref.shape[0]
    cols = n_out * PAD
    col = lax.broadcasted_iota(jnp.int32, (toks, cols), 1)
    col_expert = col // PAD
    col_slot = lax.rem(col, PAD)
    named = jnp.zeros((toks, cols), F32)
    weight = jnp.zeros((toks, cols), F32)
    for k in range(ids_ref.shape[1]):
        hit = ids_ref[:, k : k + 1] == col_expert
        named = named + jnp.where(hit, 1.0, 0.0)
        weight = weight + jnp.where(hit, scale_ref[:, k : k + 1], 0.0)
    earlier = jnp.where(
        lax.broadcasted_iota(jnp.int32, (toks, toks), 0)
        > lax.broadcasted_iota(jnp.int32, (toks, toks), 1),
        1.0,
        0.0,
    ).astype(BF)
    position = dot(earlier, named.astype(BF), NN)
    chosen = jnp.where(position == col_slot.astype(F32), named, 0.0)
    place[...] = chosen.astype(BF)
    slot_scale = jnp.sum(jnp.transpose(chosen * weight), axis=1, keepdims=True)
    place_t = jnp.transpose(chosen).astype(BF)

    cw = 1024
    n_c = width // cw

    def span(j, w=cw):
        return pl.ds(pl.multiple_of(j * w, w), w)

    def pick(a):
        def step(j, carry):
            v = dot(place_t, tok[a, :, span(j)], NN)
            if a == 1:
                v = v * slot_scale
            ysend[a, :, :, span(j)] = v.astype(BF).reshape(n_out, PAD, cw)
            return carry

        lax.fori_loop(0, n_c, step, 0)
        yrecv[a, me_o] = ysend[a, me_o]

    def y_copy(a, d):
        return pltpu.make_async_remote_copy(
            src_ref=ysend.at[a, peer(d)],
            dst_ref=yrecv.at[a, me_o],
            send_sem=y_send_sem.at[a, d],
            recv_sem=y_recv_sem.at[a, d],
            device_id=(peer(d), me_i),
            device_id_type=MESH,
        )

    y_copies = [[y_copy(a, d) for d in range(1, n_out)] for a in range(2)]
    loads[0].wait()
    pick(0)
    pl.semaphore_wait(barrier, len(plane) + n_out - 1)
    for c in y_copies[0]:
        c.start()
    loads[1].wait()
    pick(1)
    for c in y_copies[1]:
        c.start()

    row = lax.broadcasted_iota(jnp.int32, (slots, cols), 0)
    pcol = lax.broadcasted_iota(jnp.int32, (slots, cols), 1)
    compact = jnp.where((row // CAP) * PAD + lax.rem(row, CAP) == pcol, 1.0, 0.0).astype(BF)

    def gather_own(a):
        for d in range(1, n_out):
            pltpu.make_async_remote_copy(
                src_ref=ysend.at[a, 0],
                dst_ref=yrecv.at[a, lax.rem(me_o + n_out - d, n_out)],
                send_sem=y_send_sem.at[a, d],
                recv_sem=y_recv_sem.at[a, d],
                device_id=(peer(d), me_i),
                device_id_type=MESH,
            ).wait_recv()

        def step(j, carry):
            v = yrecv[a, :, :, span(j)].reshape(cols, cw)
            rows[a, me_i, :, span(j)] = dot(compact, v, NN).astype(BF)
            return carry

        lax.fori_loop(0, n_c, step, 0)

    started = []

    def piece(a, f, s, h):
        ref = rows.at[a, block(a, f, s)]
        return ref if h is None else ref.at[:, pl.ds(h * half, half)]

    def ag(a, k, f, s, h, f_to, s_to):
        c = pltpu.make_async_remote_copy(
            src_ref=piece(a, f, s, h),
            dst_ref=piece(a, f, s, h),
            send_sem=ag_send.at[a, k],
            recv_sem=ag_recv.at[a, k],
            device_id=(me_o, block(a, f_to, s_to)),
            device_id_type=MESH,
        )
        c.start()
        started.append(c)

    def ag_wait(a, k, f, s, h):
        pltpu.make_async_remote_copy(
            src_ref=piece(a, f, s, h),
            dst_ref=piece(a, f, s, h),
            send_sem=ag_send.at[a, k],
            recv_sem=ag_recv.at[a, k],
            device_id=(me_o, block(a, first[a], second[a])),
            device_id_type=MESH,
        ).wait_recv()

    def out_second(a, off):
        f, s = first[a], second[a]
        ag(a, 4 + off, ring(f, off), s, None, f, ring(s, 1))
        ag(a, 8 + off, ring(f, off), s, None, f, ring(s, 3))

    def on_second_plus(a, off):
        f, s = ring(first[a], off), second[a]
        ag_wait(a, 4 + off, f, ring(s, 3), None)
        ag(a, 12 + off, f, ring(s, 3), 0, first[a], ring(s, 1))

    def on_second_minus(a, off):
        f, s = ring(first[a], off), second[a]
        ag_wait(a, 8 + off, f, ring(s, 1), None)
        ag(a, 16 + off, f, ring(s, 1), 1, first[a], ring(s, 3))

    def on_second_far(a, off):
        f, s = ring(first[a], off), second[a]
        ag_wait(a, 12 + off, f, ring(s, 2), 0)
        ag_wait(a, 16 + off, f, ring(s, 2), 1)

    def round0(a):
        f, s = first[a], second[a]
        ag(a, 0, f, s, None, ring(f, 1), s)
        ag(a, 1, f, s, None, ring(f, 3), s)
        out_second(a, 0)

    def round1(a):
        f, s = first[a], second[a]
        ag_wait(a, 0, ring(f, 3), s, None)
        ag(a, 2, ring(f, 3), s, 0, ring(f, 1), s)
        out_second(a, 3)
        ag_wait(a, 1, ring(f, 1), s, None)
        ag(a, 3, ring(f, 1), s, 1, ring(f, 3), s)
        out_second(a, 1)
        on_second_plus(a, 0)
        on_second_minus(a, 0)

    def round2(a):
        f, s = first[a], second[a]
        ag_wait(a, 2, ring(f, 2), s, 0)
        ag_wait(a, 3, ring(f, 2), s, 1)
        out_second(a, 2)
        for off in (3, 1):
            on_second_plus(a, off)
            on_second_minus(a, off)

    def round3(a):
        on_second_plus(a, 2)
        on_second_minus(a, 2)

    def forward(a, blocks):
        for off_f, off_s in blocks:
            b = block(a, ring(first[a], off_f), ring(second[a], off_s))
            if a == 0:

                def step(j, acc, b=b):
                    return acc + dot(rows[0, b, :, span(j)], wgu[span(j), :], NN)

                gu[b] = lax.fori_loop(0, n_c, step, jnp.zeros((slots, 256), F32))
            else:

                def step(j, acc, b=b):
                    return acc + dot(rows[1, b, :, span(j)], wd[:, span(j)], NT)

                hid[b] = lax.fori_loop(0, n_c, step, jnp.zeros((slots, 128), F32))

    gather_own(0)
    round0(0)
    gather_own(1)
    round0(1)
    for c in loads[2:]:
        c.wait()
    for a in range(2):
        forward(a, [(0, 0)])
    round1(0)
    round1(1)
    for a in range(2):
        forward(a, [(1, 0), (3, 0), (0, 1), (0, 3)])
    round2(0)
    round2(1)
    for a in range(2):
        on_second_far(a, 0)
        forward(a, [(2, 0), (1, 1), (3, 1), (1, 3), (3, 3), (0, 2)])
    round3(0)
    round3(1)
    for a in range(2):
        on_second_far(a, 1)
        on_second_far(a, 3)
        forward(a, [(2, 1), (2, 3), (1, 2), (3, 2)])
    for a in range(2):
        on_second_far(a, 2)
        forward(a, [(2, 2)])

    def nonlinear(b, carry):
        gate = gu[b, :, 0:128]
        up = gu[b, :, 128:256]
        grad = hid[b]
        sig = jax.nn.sigmoid(gate)
        silu = gate * sig
        act[b] = (silu * up).astype(BF)
        ggug[b, :, 0:128] = (grad * up * sig * (1.0 + gate * (1.0 - sig))).astype(BF)
        ggug[b, :, 128:256] = (grad * silu).astype(BF)
        return carry

    lax.fori_loop(0, SIDE * SIDE, nonlinear, 0)

    tw = 512
    n_t = half // tw
    p_of = (my_z, my_x)
    q_of = (my_x, my_z)

    def rs_block(a, p, q):
        return p * SIDE + q if a == 0 else q * SIDE + p

    def rs_dev(a, p, q):
        return (me_o, rs_block(a, p, q))

    def rs_copy(a, k, src, dst, p, q):
        return pltpu.make_async_remote_copy(
            src_ref=src,
            dst_ref=dst,
            send_sem=rs_send.at[a, k],
            recv_sem=rs_recv.at[a, k],
            device_id=rs_dev(a, p, q),
            device_id_type=MESH,
        )

    def terms(a, p, qs, put):
        m = jnp.concatenate([ggug[rs_block(a, p, q)] for q in qs], axis=0)

        def step(j, carry):
            w = wgu[pl.ds(pl.multiple_of(a * half + j * tw, tw), tw), :]
            v = dot(m, w, NT).reshape(len(qs), slots, tw)
            put(v, span(j, tw))
            return carry

        lax.fori_loop(0, n_t, step, 0)

    lo, hi = pl.ds(0, 2), pl.ds(2, 2)

    def phase_copies(a):
        p, q = p_of[a], q_of[a]
        up, dn = (ring(p, 1), q), (ring(p, 3), q)
        qu, qd = (p, ring(q, 1)), (p, ring(q, 3))
        c0, c1 = pl.ds(0, quarter), pl.ds(quarter, quarter)
        far, nxt, prv = part.at[a, ring(q, 2)], part.at[a, ring(q, 1)], part.at[a, ring(q, 3)]
        return [
            rs_copy(a, 0, sf.at[a, 0], rf.at[a, 0], *up),
            rs_copy(a, 1, sf.at[a, 1], rf.at[a, 1], *dn),
            rs_copy(a, 2, sn.at[a, 0, hi], rn.at[a, 0, hi], *up),
            rs_copy(a, 3, sn.at[a, 1, lo], rn.at[a, 1, lo], *dn),
            rs_copy(a, 4, sn.at[a, 0, lo], rn.at[a, 0, lo], *up),
            rs_copy(a, 5, sn.at[a, 1, hi], rn.at[a, 1, hi], *dn),
            rs_copy(a, 6, far.at[:, c0], rf2.at[a, 0], *qu),
            rs_copy(a, 7, far.at[:, c1], rf2.at[a, 1], *qd),
            rs_copy(a, 8, nxt.at[:, c1], rn2.at[a, 0, :, c1], *qu),
            rs_copy(a, 9, prv.at[:, c0], rn2.at[a, 1, :, c0], *qd),
            rs_copy(a, 10, nxt.at[:, c0], rn2.at[a, 0, :, c0], *qu),
            rs_copy(a, 11, prv.at[:, c1], rn2.at[a, 1, :, c1], *qd),
        ]

    rs = [phase_copies(a) for a in range(2)]

    for a in range(2):

        def put_far(v, s, a=a):
            sf[a, 0, :, :, s] = v[0:2].astype(BF)
            sf[a, 1, :, :, s] = v[2:4].astype(BF)

        terms(a, ring(p_of[a], 2), (0, 1, 2, 3), put_far)
        rs[a][0].start()
        rs[a][1].start()
    for a in range(2):

        def put_up(v, s, a=a):
            sn[a, 0, 2:4, :, s] = v.astype(BF)

        def put_dn(v, s, a=a):
            sn[a, 1, 0:2, :, s] = v.astype(BF)

        terms(a, ring(p_of[a], 1), (2, 3), put_up)
        rs[a][2].start()
        terms(a, ring(p_of[a], 3), (0, 1), put_dn)
        rs[a][3].start()

    gw = 512

    def grad_step(j, carry):
        slot = lax.rem(j, 2)

        def outs(i):
            dst = pl.ds(pl.multiple_of(i * gw, gw), gw)
            return (
                pltpu.make_async_copy(
                    stage.at[slot, :, pl.ds(0, 128)], gate_hbm.at[dst, :], out_sem.at[0, slot]
                ),
                pltpu.make_async_copy(
                    stage.at[slot, :, pl.ds(128, 128)], up_hbm.at[dst, :], out_sem.at[1, slot]
                ),
            )

        @pl.when(j >= 2)
        def _():
            for c in outs(j - 2):
                c.wait()

        xs = rows[0, :, :, span(j, gw)].reshape(SIDE * SIDE * slots, gw)
        stage[slot] = dot(xs, ggug[...].reshape(SIDE * SIDE * slots, 256), TN)
        for c in outs(j):
            c.start()
        return carry

    def down_step(j, carry):
        slot = lax.rem(j, 2)

        def out(i):
            return pltpu.make_async_copy(
                stage_d.at[slot], down_hbm.at[:, span(i, gw)], out_d_sem.at[slot]
            )

        @pl.when(j >= 2)
        def _():
            out(j - 2).wait()

        gs = rows[1, :, :, span(j, gw)].reshape(SIDE * SIDE * slots, gw)
        stage_d[slot] = dot(act[...].reshape(SIDE * SIDE * slots, 128), gs, TN)
        out(j).start()
        return carry

    n_g = width // gw
    lax.fori_loop(0, n_g, down_step, 0)

    for a in range(2):

        def put_up2(v, s, a=a):
            sn[a, 0, 0:2, :, s] = (v + rf[a, 0, :, :, s].astype(F32)).astype(BF)

        def put_dn2(v, s, a=a):
            sn[a, 1, 2:4, :, s] = (v + rf[a, 1, :, :, s].astype(F32)).astype(BF)

        rs[a][0].wait_recv()
        terms(a, ring(p_of[a], 1), (0, 1), put_up2)
        rs[a][4].start()
        rs[a][1].wait_recv()
        terms(a, ring(p_of[a], 3), (2, 3), put_dn2)
        rs[a][5].start()

    lax.fori_loop(0, n_g, grad_step, 0)

    for a in range(2):
        for k in (2, 3, 4, 5):
            rs[a][k].wait_recv()

        def put_part(v, s, a=a):
            t = v + rn[a, 0, :, :, s].astype(F32) + rn[a, 1, :, :, s].astype(F32)
            part[a, :, :, s] = t.astype(BF)

        terms(a, p_of[a], (0, 1, 2, 3), put_part)
        for k in (6, 7, 8, 9):
            rs[a][k].start()
    for a in range(2):
        q = q_of[a]
        c0, c1 = pl.ds(0, quarter), pl.ds(quarter, quarter)
        for k, off, c, r in ((6, 1, c0, 0), (7, 3, c1, 1)):
            rs[a][k].wait_recv()
            b = ring(q, off)
            t = part[a, b, :, c].astype(F32) + rf2[a, r].astype(F32)
            part[a, b, :, c] = t.astype(BF)
            rs[a][k + 4].start()
    for a in range(2):
        for k in (8, 9, 10, 11):
            rs[a][k].wait_recv()
        t = part[a, q_of[a]].astype(F32) + rn2[a, 0].astype(F32) + rn2[a, 1].astype(F32)
        final[:, pl.ds(a * half, half)] = t.astype(BF)

    for c in y_copies[0]:
        c.wait_send()
    spread = jnp.where(
        (lax.broadcasted_iota(jnp.int32, (cols, slots), 1) // CAP) * PAD
        + lax.rem(lax.broadcasted_iota(jnp.int32, (cols, slots), 1), CAP)
        == lax.broadcasted_iota(jnp.int32, (cols, slots), 0),
        1.0,
        0.0,
    ).astype(BF)

    def spread_step(j, carry):
        v = dot(spread, final[:, span(j)], NN).astype(BF)
        ysend[0, :, :, span(j)] = v.reshape(n_out, PAD, cw)
        return carry

    lax.fori_loop(0, n_c, spread_step, 0)
    back_copies = []
    for d in range(1, n_out):
        c = pltpu.make_async_remote_copy(
            src_ref=ysend.at[0, peer(d)],
            dst_ref=back.at[me_o],
            send_sem=b_send_sem.at[d],
            recv_sem=b_recv_sem.at[d],
            device_id=(peer(d), me_i),
            device_id_type=MESH,
        )
        c.start()
        back_copies.append(c)
    back[me_o] = ysend[0, me_o]
    for d in range(1, n_out):
        pltpu.make_async_remote_copy(
            src_ref=ysend.at[0, 0],
            dst_ref=back.at[lax.rem(me_o + n_out - d, n_out)],
            send_sem=b_send_sem.at[d],
            recv_sem=b_recv_sem.at[d],
            device_id=(peer(d), me_i),
            device_id_type=MESH,
        ).wait_recv()

    def in_step(j, carry):
        v = back[:, :, span(j)].reshape(cols, cw)
        tok[0, :, span(j)] = dot(place[...], v, NN).astype(BF)
        return carry

    lax.fori_loop(0, n_c, in_step, 0)
    in_out = pltpu.make_async_copy(tok.at[0], in_grad_hbm, load_sem.at[0])
    in_out.start()

    for c in started:
        c.wait_send()
    for c in y_copies[1]:
        c.wait_send()
    for c in back_copies:
        c.wait_send()
    for a in range(2):
        for c in rs[a]:
            c.wait_send()
    for i in (n_g - 2, n_g - 1):
        slot = i % 2
        dst = pl.ds(i * gw, gw)
        pltpu.make_async_copy(
            stage.at[slot, :, pl.ds(0, 128)], gate_hbm.at[dst, :], out_sem.at[0, slot]
        ).wait()
        pltpu.make_async_copy(
            stage.at[slot, :, pl.ds(128, 128)], up_hbm.at[dst, :], out_sem.at[1, slot]
        ).wait()
        pltpu.make_async_copy(
            stage_d.at[slot], down_hbm.at[:, dst], out_d_sem.at[slot]
        ).wait()
    in_out.wait()


def shards(layer_input, out_grad, expert_ids, route_scales, w_gate, w_up, w_down):
    toks, width = layer_input.shape
    n_out = lax.axis_size("outer")
    n_in = lax.axis_size("inner")
    hidden = w_gate.shape[2]
    slots = n_out * CAP
    half, quarter = width // 2, width // 4
    any_spec = pl.BlockSpec(memory_space=pl.ANY)
    vmem = pl.BlockSpec(memory_space=pltpu.VMEM)
    dma = pltpu.SemaphoreType.DMA
    in_grad, gate, up, down = pl.pallas_call(
        kernel,
        out_shape=(
            jax.ShapeDtypeStruct((toks, width), BF),
            jax.ShapeDtypeStruct((width, hidden), F32),
            jax.ShapeDtypeStruct((width, hidden), F32),
            jax.ShapeDtypeStruct((hidden, width), F32),
        ),
        in_specs=[vmem, vmem] + [any_spec] * 5,
        out_specs=(any_spec,) * 4,
        scratch_shapes=[
            pltpu.VMEM((2, toks, width), BF),
            pltpu.VMEM((width, 2 * hidden), BF),
            pltpu.VMEM((hidden, width), BF),
            pltpu.VMEM((toks, n_out * PAD), BF),
            pltpu.VMEM((2, n_out, PAD, width), BF),
            pltpu.VMEM((2, n_out, PAD, width), BF),
            pltpu.VMEM((n_out, PAD, width), BF),
            pltpu.VMEM((2, n_in, slots, width), BF),
            pltpu.VMEM((n_in, slots, 2 * hidden), F32),
            pltpu.VMEM((n_in, slots, hidden), F32),
            pltpu.VMEM((n_in, slots, 2 * hidden), BF),
            pltpu.VMEM((n_in, slots, hidden), BF),
            pltpu.VMEM((2, 2, 2, slots, half), BF),
            pltpu.VMEM((2, 2, 2, slots, half), BF),
            pltpu.VMEM((2, 2, SIDE, slots, half), BF),
            pltpu.VMEM((2, 2, SIDE, slots, half), BF),
            pltpu.VMEM((2, SIDE, slots, half), BF),
            pltpu.VMEM((2, 2, slots, quarter), BF),
            pltpu.VMEM((2, 2, slots, half), BF),
            pltpu.VMEM((slots, width), BF),
            pltpu.VMEM((2, 512, 2 * hidden), F32),
            pltpu.VMEM((2, hidden, 512), F32),
            dma((5,)),
            dma((2, n_out)),
            dma((2, n_out)),
            dma((n_out,)),
            dma((n_out,)),
            dma((2, 20)),
            dma((2, 20)),
            dma((2, 12)),
            dma((2, 12)),
            dma((2, 2)),
            dma((2,)),
        ],
        compiler_params=pltpu.CompilerParams(
            collective_id=0, has_side_effects=True, vmem_limit_bytes=67043328
        ),
        name="expert_backward",
    )(expert_ids, route_scales, layer_input, out_grad, w_gate[0], w_up[0], w_down[0])
    return in_grad, gate[None], up[None], down[None]


def solution(mesh):
    return jax.shard_map(
        shards,
        mesh=mesh,
        in_specs=(
            P(("outer", "inner"), None),
            P(("outer", "inner"), None),
            P(("outer", "inner"), None),
            P(("outer", "inner"), None),
            P("outer", None, "inner"),
            P("outer", None, "inner"),
            P("outer", "inner", None),
        ),
        out_specs=(
            P(("outer", "inner"), None),
            P("outer", None, "inner"),
            P("outer", None, "inner"),
            P("outer", "inner", None),
        ),
        check_vma=False,
    )
```

```python
import jax
import jax.numpy as jnp
from jax import lax
from jax.experimental import pallas as pl
from jax.experimental.pallas import tpu as pltpu
from jax.sharding import PartitionSpec as P

CAP = 6
PAD = 8
SIDE = 4
BF = jnp.bfloat16
F32 = jnp.float32
MESH = pl.DeviceIdType.MESH
NN = (((1,), (0,)), ((), ()))
NT = (((1,), (1,)), ((), ()))
TN = (((0,), (0,)), ((), ()))


def dot(a, b, dims):
    return lax.dot_general(a, b, dims, preferred_element_type=F32)


def kernel(
    ids_ref, scale_ref, x_hbm, dy_hbm, wg_hbm, wu_hbm, wd_hbm,
    back_hbm, place_hbm, gate_hbm, up_hbm, down_hbm,
    tok, wgu, wd, place, ysend, yrecv, back, rows, gu, hid, ggug, act,
    sf, rf, sn, rn, part, rf2, rn2, stage, stage_d,
    load_sem, y_send_sem, y_recv_sem, b_send_sem, b_recv_sem,
    ag_send, ag_recv, rs_send, rs_recv, out_sem, out_d_sem, b_out_sem, place_sem,
):
    n_out = ysend.shape[1]
    width = tok.shape[2]
    half = width // 2
    quarter = width // 4
    eighth = width // 8
    slots = n_out * CAP
    me_o = lax.axis_index("outer")
    me_i = lax.axis_index("inner")
    my_z = me_i // SIDE
    my_x = lax.rem(me_i, SIDE)

    def ring(v, k):
        return lax.rem(v + k, SIDE)

    def peer(d):
        return lax.rem(me_o + d, n_out)

    first = (my_x, my_z)
    second = (my_z, my_x)

    def block(a, f, s):
        return s * SIDE + f if a == 0 else f * SIDE + s

    barrier = pltpu.get_barrier_semaphore()
    plane = [
        my_z * SIDE + ring(my_x, 1), my_z * SIDE + ring(my_x, 3),
        ring(my_z, 1) * SIDE + my_x, ring(my_z, 3) * SIDE + my_x,
    ]
    for i in plane:
        pl.semaphore_signal(barrier, inc=1, device_id=(me_o, i), device_id_type=MESH)
    for d in range(1, n_out):
        pl.semaphore_signal(barrier, inc=1, device_id=(peer(d), me_i), device_id_type=MESH)

    loads = [
        pltpu.make_async_copy(x_hbm, tok.at[0], load_sem.at[0]),
        pltpu.make_async_copy(dy_hbm, tok.at[1], load_sem.at[1]),
        pltpu.make_async_copy(wg_hbm, wgu.at[:, pl.ds(0, 128)], load_sem.at[2]),
        pltpu.make_async_copy(wu_hbm, wgu.at[:, pl.ds(128, 128)], load_sem.at[3]),
        pltpu.make_async_copy(wd_hbm, wd, load_sem.at[4]),
    ]
    for c in loads:
        c.start()

    ids = jnp.transpose(ids_ref[...].astype(F32))
    scales = jnp.transpose(scale_ref[...])
    toks = ids.shape[0]
    cols = n_out * PAD
    col = lax.broadcasted_iota(jnp.int32, (toks, cols), 1)
    col_expert = (col // PAD).astype(F32)
    col_slot = lax.rem(col, PAD)
    named = jnp.zeros((toks, cols), F32)
    weight = jnp.zeros((toks, cols), F32)
    for k in range(ids.shape[1]):
        hit = ids[:, k : k + 1] == col_expert
        named = named + jnp.where(hit, 1.0, 0.0)
        weight = weight + jnp.where(hit, scales[:, k : k + 1], 0.0)
    earlier = jnp.where(
        lax.broadcasted_iota(jnp.int32, (toks, toks), 0)
        > lax.broadcasted_iota(jnp.int32, (toks, toks), 1),
        1.0,
        0.0,
    ).astype(BF)
    position = dot(earlier, named.astype(BF), NN)
    chosen = jnp.where(position == col_slot.astype(F32), named, 0.0)
    place[...] = chosen.astype(BF)
    place_out = pltpu.make_async_copy(place, place_hbm, place_sem)
    place_out.start()
    slot_scale = jnp.sum(jnp.transpose(chosen * weight), axis=1, keepdims=True)
    place_t = jnp.transpose(chosen).astype(BF)

    cw = 1024
    n_c = width // cw

    def span(j, w=cw):
        return pl.ds(pl.multiple_of(j * w, w), w)

    def part_span(first_col, j):
        return pl.ds(pl.multiple_of(first_col + j * eighth, eighth), eighth)

    def pick(a, h):
        def step(j, carry):
            s = part_span(h * half, j)
            v = dot(place_t, tok[a, :, s], NN)
            if a == 1:
                v = v * slot_scale
            ysend[a, :, :, s] = v.astype(BF).reshape(n_out, PAD, eighth)
            return carry

        lax.fori_loop(0, 4, step, 0)
        own = pl.ds(h * half, half)
        yrecv[a, me_o, :, own] = ysend[a, me_o, :, own]

    def y_copy(a, h, d):
        own = pl.ds(h * half, half)
        return pltpu.make_async_remote_copy(
            src_ref=ysend.at[a, peer(d), :, own],
            dst_ref=yrecv.at[a, me_o, :, own],
            send_sem=y_send_sem.at[a, h, d],
            recv_sem=y_recv_sem.at[a, h, d],
            device_id=(peer(d), me_i),
            device_id_type=MESH,
        )

    y_copies = [[], []]
    for a in range(2):
        loads[a].wait()
        for h in range(2):
            pick(a, h)
            if a == 0 and h == 0:
                pl.semaphore_wait(barrier, len(plane) + n_out - 1)
            for d in range(1, n_out):
                c = y_copy(a, h, d)
                c.start()
                y_copies[a].append(c)

    row = lax.broadcasted_iota(jnp.int32, (slots, cols), 0)
    pcol = lax.broadcasted_iota(jnp.int32, (slots, cols), 1)
    compact = jnp.where((row // CAP) * PAD + lax.rem(row, CAP) == pcol, 1.0, 0.0).astype(BF)

    def gather_own(a, h):
        own = pl.ds(h * half, half)
        for d in range(1, n_out):
            pltpu.make_async_remote_copy(
                src_ref=ysend.at[a, 0, :, own],
                dst_ref=yrecv.at[a, lax.rem(me_o + n_out - d, n_out), :, own],
                send_sem=y_send_sem.at[a, h, d],
                recv_sem=y_recv_sem.at[a, h, d],
                device_id=(peer(d), me_i),
                device_id_type=MESH,
            ).wait_recv()

        def step(j, carry):
            s = part_span(h * half, j)
            v = yrecv[a, :, :, s].reshape(cols, eighth)
            rows[a, me_i, :, s] = dot(compact, v, NN).astype(BF)
            return carry

        lax.fori_loop(0, 4, step, 0)

    started = []

    def piece(a, f, s, h):
        ref = rows.at[a, block(a, f, s)]
        return ref if h is None else ref.at[:, pl.ds(h * half, half)]

    def ag(a, k, f, s, h, f_to, s_to):
        c = pltpu.make_async_remote_copy(
            src_ref=piece(a, f, s, h),
            dst_ref=piece(a, f, s, h),
            send_sem=ag_send.at[a, k, h or 0],
            recv_sem=ag_recv.at[a, k, h or 0],
            device_id=(me_o, block(a, f_to, s_to)),
            device_id_type=MESH,
        )
        c.start()
        started.append(c)

    def ag_wait(a, k, f, s, h):
        pltpu.make_async_remote_copy(
            src_ref=piece(a, f, s, h),
            dst_ref=piece(a, f, s, h),
            send_sem=ag_send.at[a, k, h or 0],
            recv_sem=ag_recv.at[a, k, h or 0],
            device_id=(me_o, block(a, first[a], second[a])),
            device_id_type=MESH,
        ).wait_recv()

    def out_second(a, off):
        f, s = first[a], second[a]
        ag(a, 4 + off, ring(f, off), s, None, f, ring(s, 1))
        ag(a, 8 + off, ring(f, off), s, None, f, ring(s, 3))

    def on_second_plus(a, off):
        f, s = ring(first[a], off), second[a]
        for h in (0, 1) if off == 0 else (None,):
            ag_wait(a, 4 + off, f, ring(s, 3), h)
        ag(a, 12 + off, f, ring(s, 3), 0, first[a], ring(s, 1))

    def on_second_minus(a, off):
        f, s = ring(first[a], off), second[a]
        for h in (0, 1) if off == 0 else (None,):
            ag_wait(a, 8 + off, f, ring(s, 1), h)
        ag(a, 16 + off, f, ring(s, 1), 1, first[a], ring(s, 3))

    def on_second_far(a, off):
        f, s = ring(first[a], off), second[a]
        ag_wait(a, 12 + off, f, ring(s, 2), 0)
        ag_wait(a, 16 + off, f, ring(s, 2), 1)

    def round0(a, h):
        f, s = first[a], second[a]
        ag(a, 0, f, s, h, ring(f, 1), s)
        ag(a, 1, f, s, h, ring(f, 3), s)
        ag(a, 4, f, s, h, f, ring(s, 1))
        ag(a, 8, f, s, h, f, ring(s, 3))

    def round1(a):
        f, s = first[a], second[a]
        ag_wait(a, 0, ring(f, 3), s, 0)
        ag(a, 2, ring(f, 3), s, 0, ring(f, 1), s)
        ag_wait(a, 0, ring(f, 3), s, 1)
        out_second(a, 3)
        ag_wait(a, 1, ring(f, 1), s, 0)
        ag_wait(a, 1, ring(f, 1), s, 1)
        ag(a, 3, ring(f, 1), s, 1, ring(f, 3), s)
        out_second(a, 1)
        on_second_plus(a, 0)
        on_second_minus(a, 0)

    def round2(a):
        f, s = first[a], second[a]
        ag_wait(a, 2, ring(f, 2), s, 0)
        ag_wait(a, 3, ring(f, 2), s, 1)
        out_second(a, 2)
        for off in (3, 1):
            on_second_plus(a, off)
            on_second_minus(a, off)

    def round3(a):
        on_second_plus(a, 2)
        on_second_minus(a, 2)

    def forward(a, blocks):
        for off_f, off_s in blocks:
            b = block(a, ring(first[a], off_f), ring(second[a], off_s))
            if a == 0:

                def step(j, acc, b=b):
                    return acc + dot(rows[0, b, :, span(j)], wgu[span(j), :], NN)

                gu[b] = lax.fori_loop(0, n_c, step, jnp.zeros((slots, 256), F32))
            else:

                def step(j, acc, b=b):
                    return acc + dot(rows[1, b, :, span(j)], wd[:, span(j)], NT)

                hid[b] = lax.fori_loop(0, n_c, step, jnp.zeros((slots, 128), F32))

    for a in range(2):
        for h in range(2):
            gather_own(a, h)
            round0(a, h)
    for c in loads[2:]:
        c.wait()
    for a in range(2):
        forward(a, [(0, 0)])
    round1(0)
    round1(1)
    for a in range(2):
        forward(a, [(1, 0), (3, 0), (0, 1), (0, 3)])
    round2(0)
    round2(1)
    for a in range(2):
        on_second_far(a, 0)
        forward(a, [(2, 0), (1, 1), (3, 1), (1, 3), (3, 3), (0, 2)])
    round3(0)
    round3(1)
    for a in range(2):
        on_second_far(a, 1)
        on_second_far(a, 3)
        forward(a, [(2, 1), (2, 3), (1, 2), (3, 2)])
    def nonlinear(b, carry):
        gate = gu[b, :, 0:128]
        up = gu[b, :, 128:256]
        grad = hid[b]
        sig = jax.nn.sigmoid(gate)
        silu = gate * sig
        act[b] = (silu * up).astype(BF)
        ggug[b, :, 0:128] = (grad * up * sig * (1.0 + gate * (1.0 - sig))).astype(BF)
        ggug[b, :, 128:256] = (grad * silu).astype(BF)
        return carry

    last = ring(my_z, 2) * SIDE + ring(my_x, 2)

    def nonlinear_early(j, carry):
        return nonlinear(lax.rem(last + j, SIDE * SIDE), carry)

    lax.fori_loop(1, SIDE * SIDE, nonlinear_early, 0)

    p_of = (my_z, my_x)
    q_of = (my_x, my_z)

    def rs_block(a, p, q):
        return p * SIDE + q if a == 0 else q * SIDE + p

    def rs_dev(a, p, q):
        return (me_o, rs_block(a, p, q))

    def rs_copy(a, c, k, src, dst, p, q):
        return pltpu.make_async_remote_copy(
            src_ref=src,
            dst_ref=dst,
            send_sem=rs_send.at[a, c, k],
            recv_sem=rs_recv.at[a, c, k],
            device_id=rs_dev(a, p, q),
            device_id_type=MESH,
        )

    def terms(a, c, p, qs, put):
        m = jnp.concatenate([ggug[rs_block(a, p, q)] for q in qs], axis=0)

        def step(j, carry):
            w = wgu[part_span(a * half + c * quarter, j), :]
            v = dot(m, w, NT).reshape(len(qs), slots, eighth)
            put(v, part_span(c * quarter, j))
            return carry

        lax.fori_loop(0, 2, step, 0)

    lo, hi = pl.ds(0, 2), pl.ds(2, 2)

    def phase_copies(a, c):
        p, q = p_of[a], q_of[a]
        up, dn = (ring(p, 1), q), (ring(p, 3), q)
        qu, qd = (p, ring(q, 1)), (p, ring(q, 3))
        cc = pl.ds(c * quarter, quarter)
        c0, c1 = pl.ds(c * quarter, eighth), pl.ds(c * quarter + eighth, eighth)
        ce = pl.ds(c * eighth, eighth)
        far, nxt, prv = part.at[a, ring(q, 2)], part.at[a, ring(q, 1)], part.at[a, ring(q, 3)]
        return [
            rs_copy(a, c, 0, sf.at[a, 0, :, :, cc], rf.at[a, 0, :, :, cc], *up),
            rs_copy(a, c, 1, sf.at[a, 1, :, :, cc], rf.at[a, 1, :, :, cc], *dn),
            rs_copy(a, c, 2, sn.at[a, 0, hi, :, cc], rn.at[a, 0, hi, :, cc], *up),
            rs_copy(a, c, 3, sn.at[a, 1, lo, :, cc], rn.at[a, 1, lo, :, cc], *dn),
            rs_copy(a, c, 4, sn.at[a, 0, lo, :, cc], rn.at[a, 0, lo, :, cc], *up),
            rs_copy(a, c, 5, sn.at[a, 1, hi, :, cc], rn.at[a, 1, hi, :, cc], *dn),
            rs_copy(a, c, 6, far.at[:, c0], rf2.at[a, 0, :, ce], *qu),
            rs_copy(a, c, 7, far.at[:, c1], rf2.at[a, 1, :, ce], *qd),
            rs_copy(a, c, 8, nxt.at[:, c1], rn2.at[a, 0, :, c1], *qu),
            rs_copy(a, c, 9, prv.at[:, c0], rn2.at[a, 1, :, c0], *qd),
            rs_copy(a, c, 10, nxt.at[:, c0], rn2.at[a, 0, :, c0], *qu),
            rs_copy(a, c, 11, prv.at[:, c1], rn2.at[a, 1, :, c1], *qd),
        ]

    rs = [[phase_copies(a, c) for c in range(2)] for a in range(2)]

    def near_at_once(a, c):
        def put_up(v, s):
            sn[a, 0, 2:4, :, s] = v.astype(BF)

        def put_dn(v, s):
            sn[a, 1, 0:2, :, s] = v.astype(BF)

        terms(a, c, ring(p_of[a], 1), (2, 3), put_up)
        rs[a][c][2].start()
        terms(a, c, ring(p_of[a], 3), (0, 1), put_dn)
        rs[a][c][3].start()

    def far_part(a, c):
        def put_far(v, s):
            sf[a, 0, :, :, s] = v[0:2].astype(BF)
            sf[a, 1, :, :, s] = v[2:4].astype(BF)

        terms(a, c, ring(p_of[a], 2), (0, 1, 2, 3), put_far)
        rs[a][c][0].start()
        rs[a][c][1].start()

    def near_after(a, c):
        def put_up2(v, s):
            sn[a, 0, 0:2, :, s] = (v + rf[a, 0, :, :, s].astype(F32)).astype(BF)

        def put_dn2(v, s):
            sn[a, 1, 2:4, :, s] = (v + rf[a, 1, :, :, s].astype(F32)).astype(BF)

        rs[a][c][0].wait_recv()
        terms(a, c, ring(p_of[a], 1), (0, 1), put_up2)
        rs[a][c][4].start()
        rs[a][c][1].wait_recv()
        terms(a, c, ring(p_of[a], 3), (2, 3), put_dn2)
        rs[a][c][5].start()

    for a in range(2):
        near_at_once(a, 0)
    for a in range(2):
        on_second_far(a, 2)
        forward(a, [(2, 2)])
    nonlinear(last, 0)
    for c in range(2):
        for a in range(2):
            far_part(a, c)
    for a in range(2):
        near_at_once(a, 1)

    gw = 512

    def grad_step(j, carry):
        slot = lax.rem(j, 2)

        def outs(i):
            dst = pl.ds(pl.multiple_of(i * gw, gw), gw)
            return (
                pltpu.make_async_copy(
                    stage.at[slot, :, pl.ds(0, 128)], gate_hbm.at[dst, :], out_sem.at[0, slot]
                ),
                pltpu.make_async_copy(
                    stage.at[slot, :, pl.ds(128, 128)], up_hbm.at[dst, :], out_sem.at[1, slot]
                ),
            )

        @pl.when(j >= 2)
        def _():
            for c in outs(j - 2):
                c.wait()

        xs = rows[0, :, :, span(j, gw)].reshape(SIDE * SIDE * slots, gw)
        stage[slot] = dot(xs, ggug[...].reshape(SIDE * SIDE * slots, 256), TN)
        for c in outs(j):
            c.start()
        return carry

    def down_step(j, carry):
        slot = lax.rem(j, 2)

        def out(i):
            return pltpu.make_async_copy(
                stage_d.at[slot], down_hbm.at[:, span(i, gw)], out_d_sem.at[slot]
            )

        @pl.when(j >= 2)
        def _():
            out(j - 2).wait()

        gs = rows[1, :, :, span(j, gw)].reshape(SIDE * SIDE * slots, gw)
        stage_d[slot] = dot(act[...].reshape(SIDE * SIDE * slots, 128), gs, TN)
        out(j).start()
        return carry

    n_g = width // gw
    lax.fori_loop(0, n_g, down_step, 0)
    for c in range(2):
        for a in range(2):
            near_after(a, c)
    lax.fori_loop(0, n_g, grad_step, 0)

    for c in range(2):
        for a in range(2):
            for k in (2, 3, 4, 5):
                rs[a][c][k].wait_recv()

            def put_part(v, s, a=a):
                t = v + rn[a, 0, :, :, s].astype(F32) + rn[a, 1, :, :, s].astype(F32)
                part[a, :, :, s] = t.astype(BF)

            terms(a, c, p_of[a], (0, 1, 2, 3), put_part)
            for k in (6, 7, 8, 9):
                rs[a][c][k].start()
    for c in range(2):
        ce = pl.ds(c * eighth, eighth)
        for a in range(2):
            for k, off, col0, r in ((6, 1, 0, 0), (7, 3, eighth, 1)):
                rs[a][c][k].wait_recv()
                b = ring(q_of[a], off)
                s = pl.ds(c * quarter + col0, eighth)
                t = part[a, b, :, s].astype(F32) + rf2[a, r, :, ce].astype(F32)
                part[a, b, :, s] = t.astype(BF)
                rs[a][c][k + 4].start()

    for c in y_copies[0]:
        c.wait_send()
    spread = jnp.where(
        (lax.broadcasted_iota(jnp.int32, (cols, slots), 1) // CAP) * PAD
        + lax.rem(lax.broadcasted_iota(jnp.int32, (cols, slots), 1), CAP)
        == lax.broadcasted_iota(jnp.int32, (cols, slots), 0),
        1.0,
        0.0,
    ).astype(BF)
    back_copies = []
    for c in range(2):
        for a in range(2):
            for k in (8, 9, 10, 11):
                rs[a][c][k].wait_recv()
            first_col = a * half + c * quarter

            def final_step(j, carry, a=a, c=c, first_col=first_col):
                s = part_span(c * quarter, j)
                t = part[a, q_of[a], :, s].astype(F32) + rn2[a, 0, :, s].astype(F32)
                t = (t + rn2[a, 1, :, s].astype(F32)).astype(BF)
                v = dot(spread, t, NN).astype(BF).reshape(n_out, PAD, eighth)
                ysend[0, :, :, part_span(first_col, j)] = v
                return carry

            lax.fori_loop(0, 2, final_step, 0)
            seg = pl.ds(first_col, quarter)
            for d in range(1, n_out):
                copy = pltpu.make_async_remote_copy(
                    src_ref=ysend.at[0, peer(d), :, seg],
                    dst_ref=back.at[me_o, :, seg],
                    send_sem=b_send_sem.at[a, c, d],
                    recv_sem=b_recv_sem.at[a, c, d],
                    device_id=(peer(d), me_i),
                    device_id_type=MESH,
                )
                copy.start()
                back_copies.append(copy)
            back[me_o, :, seg] = ysend[0, me_o, :, seg]
    back_outs = []
    for c in range(2):
        for a in range(2):
            seg = pl.ds(a * half + c * quarter, quarter)
            for d in range(1, n_out):
                pltpu.make_async_remote_copy(
                    src_ref=ysend.at[0, 0, :, seg],
                    dst_ref=back.at[lax.rem(me_o + n_out - d, n_out), :, seg],
                    send_sem=b_send_sem.at[a, c, d],
                    recv_sem=b_recv_sem.at[a, c, d],
                    device_id=(peer(d), me_i),
                    device_id_type=MESH,
                ).wait_recv()
            copy = pltpu.make_async_copy(
                back.at[:, :, seg], back_hbm.at[:, :, seg], b_out_sem.at[a, c]
            )
            copy.start()
            back_outs.append(copy)

    for c in started:
        c.wait_send()
    for c in y_copies[1]:
        c.wait_send()
    for c in back_copies:
        c.wait_send()
    for a in range(2):
        for chunk in rs[a]:
            for c in chunk:
                c.wait_send()
    for i in (n_g - 2, n_g - 1):
        slot = i % 2
        dst = pl.ds(i * gw, gw)
        pltpu.make_async_copy(
            stage.at[slot, :, pl.ds(0, 128)], gate_hbm.at[dst, :], out_sem.at[0, slot]
        ).wait()
        pltpu.make_async_copy(
            stage.at[slot, :, pl.ds(128, 128)], up_hbm.at[dst, :], out_sem.at[1, slot]
        ).wait()
        pltpu.make_async_copy(
            stage_d.at[slot], down_hbm.at[:, dst], out_d_sem.at[slot]
        ).wait()
    for c in back_outs:
        c.wait()
    place_out.wait()


def shards(layer_input, out_grad, expert_ids, route_scales, w_gate, w_up, w_down):
    toks, width = layer_input.shape
    n_out = lax.axis_size("outer")
    n_in = lax.axis_size("inner")
    hidden = w_gate.shape[2]
    slots = n_out * CAP
    half, quarter = width // 2, width // 4
    any_spec = pl.BlockSpec(memory_space=pl.ANY)
    vmem = pl.BlockSpec(memory_space=pltpu.VMEM)
    dma = pltpu.SemaphoreType.DMA
    back, place, gate, up, down = pl.pallas_call(
        kernel,
        out_shape=(
            jax.ShapeDtypeStruct((n_out, PAD, width), BF),
            jax.ShapeDtypeStruct((toks, n_out * PAD), BF),
            jax.ShapeDtypeStruct((width, hidden), F32),
            jax.ShapeDtypeStruct((width, hidden), F32),
            jax.ShapeDtypeStruct((hidden, width), F32),
        ),
        in_specs=[vmem, vmem] + [any_spec] * 5,
        out_specs=(any_spec,) * 5,
        scratch_shapes=[
            pltpu.VMEM((2, toks, width), BF),
            pltpu.VMEM((width, 2 * hidden), BF),
            pltpu.VMEM((hidden, width), BF),
            pltpu.VMEM((toks, n_out * PAD), BF),
            pltpu.VMEM((2, n_out, PAD, width), BF),
            pltpu.VMEM((2, n_out, PAD, width), BF),
            pltpu.VMEM((n_out, PAD, width), BF),
            pltpu.VMEM((2, n_in, slots, width), BF),
            pltpu.VMEM((n_in, slots, 2 * hidden), F32),
            pltpu.VMEM((n_in, slots, hidden), F32),
            pltpu.VMEM((n_in, slots, 2 * hidden), BF),
            pltpu.VMEM((n_in, slots, hidden), BF),
            pltpu.VMEM((2, 2, 2, slots, half), BF),
            pltpu.VMEM((2, 2, 2, slots, half), BF),
            pltpu.VMEM((2, 2, SIDE, slots, half), BF),
            pltpu.VMEM((2, 2, SIDE, slots, half), BF),
            pltpu.VMEM((2, SIDE, slots, half), BF),
            pltpu.VMEM((2, 2, slots, quarter), BF),
            pltpu.VMEM((2, 2, slots, half), BF),
            pltpu.VMEM((2, 512, 2 * hidden), F32),
            pltpu.VMEM((2, hidden, 512), F32),
            dma((5,)),
            dma((2, 2, n_out)),
            dma((2, 2, n_out)),
            dma((2, 2, n_out)),
            dma((2, 2, n_out)),
            dma((2, 20, 2)),
            dma((2, 20, 2)),
            dma((2, 2, 12)),
            dma((2, 2, 12)),
            dma((2, 2)),
            dma((2,)),
            dma((2, 2)),
            dma,
        ],
        compiler_params=pltpu.CompilerParams(
            collective_id=0, has_side_effects=True, vmem_limit_bytes=67043328
        ),
        name="expert_backward",
    )(expert_ids.T, route_scales.T, layer_input, out_grad, w_gate[0], w_up[0], w_down[0])
    in_grad = dot(place, back.reshape(n_out * PAD, width), NN).astype(BF)
    return in_grad, gate[None], up[None], down[None]


def solution(mesh):
    return jax.shard_map(
        shards,
        mesh=mesh,
        in_specs=(
            P(("outer", "inner"), None),
            P(("outer", "inner"), None),
            P(("outer", "inner"), None),
            P(("outer", "inner"), None),
            P("outer", None, "inner"),
            P("outer", None, "inner"),
            P("outer", "inner", None),
        ),
        out_specs=(
            P(("outer", "inner"), None),
            P("outer", None, "inner"),
            P("outer", None, "inner"),
            P("outer", "inner", None),
        ),
        check_vma=False,
    )
```

```python
import jax
import jax.numpy as jnp
from jax import lax
from jax.experimental import pallas as pl
from jax.experimental.pallas import tpu as pltpu
from jax.sharding import PartitionSpec as P

CAP = 6
PAD = 8
SIDE = 4
BF = jnp.bfloat16
F32 = jnp.float32
MESH = pl.DeviceIdType.MESH
NN = (((1,), (0,)), ((), ()))
NT = (((1,), (1,)), ((), ()))
TN = (((0,), (0,)), ((), ()))


def dot(a, b, dims):
    return lax.dot_general(a, b, dims, preferred_element_type=F32)


def kernel(
    ids_ref, scale_ref, x_hbm, dy_hbm, wg_hbm, wu_hbm, wd_hbm,
    back_hbm, place_hbm, gate_hbm, up_hbm, down_hbm,
    tok, wgu, wd, place, ysend, yrecv, back, rows, gu, hid, ggug, act,
    sf, rf, sn, rn, part, rf2, rn2, stage, stage_d,
    load_sem, y_send_sem, y_recv_sem, b_send_sem, b_recv_sem,
    ag_send, ag_recv, rs_send, rs_recv, out_sem, out_d_sem, b_out_sem, place_sem,
):
    n_out = ysend.shape[1]
    width = tok.shape[2]
    half = width // 2
    quarter = width // 4
    eighth = width // 8
    slots = n_out * CAP
    me_o = lax.axis_index("outer")
    me_i = lax.axis_index("inner")
    my_z = me_i // SIDE
    my_x = lax.rem(me_i, SIDE)

    def ring(v, k):
        return lax.rem(v + k, SIDE)

    def peer(d):
        return lax.rem(me_o + d, n_out)

    first = (my_x, my_z)
    second = (my_z, my_x)

    def block(a, f, s):
        return s * SIDE + f if a == 0 else f * SIDE + s

    barrier = pltpu.get_barrier_semaphore()
    plane = [
        my_z * SIDE + ring(my_x, 1), my_z * SIDE + ring(my_x, 3),
        ring(my_z, 1) * SIDE + my_x, ring(my_z, 3) * SIDE + my_x,
    ]
    for i in plane:
        pl.semaphore_signal(barrier, inc=1, device_id=(me_o, i), device_id_type=MESH)
    for d in range(1, n_out):
        pl.semaphore_signal(barrier, inc=1, device_id=(peer(d), me_i), device_id_type=MESH)

    loads = [
        pltpu.make_async_copy(x_hbm, tok.at[0], load_sem.at[0]),
        pltpu.make_async_copy(dy_hbm, tok.at[1], load_sem.at[1]),
        pltpu.make_async_copy(wg_hbm, wgu.at[:, pl.ds(0, 128)], load_sem.at[2]),
        pltpu.make_async_copy(wu_hbm, wgu.at[:, pl.ds(128, 128)], load_sem.at[3]),
        pltpu.make_async_copy(wd_hbm, wd, load_sem.at[4]),
    ]
    for c in loads[:2]:
        c.start()

    ids = jnp.transpose(ids_ref[...].astype(F32))
    scales = jnp.transpose(scale_ref[...])
    toks = ids.shape[0]
    cols = n_out * PAD
    col = lax.broadcasted_iota(jnp.int32, (toks, cols), 1)
    col_expert = (col // PAD).astype(F32)
    col_slot = lax.rem(col, PAD)
    named = jnp.zeros((toks, cols), F32)
    weight = jnp.zeros((toks, cols), F32)
    for k in range(ids.shape[1]):
        hit = ids[:, k : k + 1] == col_expert
        named = named + jnp.where(hit, 1.0, 0.0)
        weight = weight + jnp.where(hit, scales[:, k : k + 1], 0.0)
    earlier = jnp.where(
        lax.broadcasted_iota(jnp.int32, (toks, toks), 0)
        > lax.broadcasted_iota(jnp.int32, (toks, toks), 1),
        1.0,
        0.0,
    ).astype(BF)
    position = dot(earlier, named.astype(BF), NN)
    chosen = jnp.where(position == col_slot.astype(F32), named, 0.0)
    place[...] = chosen.astype(BF)
    place_out = pltpu.make_async_copy(place, place_hbm, place_sem)
    place_out.start()
    slot_scale = jnp.sum(jnp.transpose(chosen * weight), axis=1, keepdims=True)
    place_t = jnp.transpose(chosen).astype(BF)

    cw = 1024
    n_c = width // cw

    def span(j, w=cw):
        return pl.ds(pl.multiple_of(j * w, w), w)

    def part_span(first_col, j):
        return pl.ds(pl.multiple_of(first_col + j * eighth, eighth), eighth)

    def pick(a, h):
        def step(j, carry):
            s = part_span(h * half, j)
            v = dot(place_t, tok[a, :, s], NN)
            if a == 1:
                v = v * slot_scale
            ysend[a, :, :, s] = v.astype(BF).reshape(n_out, PAD, eighth)
            return carry

        lax.fori_loop(0, 4, step, 0)
        own = pl.ds(h * half, half)
        yrecv[a, me_o, :, own] = ysend[a, me_o, :, own]

    def y_copy(a, h, d):
        own = pl.ds(h * half, half)
        return pltpu.make_async_remote_copy(
            src_ref=ysend.at[a, peer(d), :, own],
            dst_ref=yrecv.at[a, me_o, :, own],
            send_sem=y_send_sem.at[a, h, d],
            recv_sem=y_recv_sem.at[a, h, d],
            device_id=(peer(d), me_i),
            device_id_type=MESH,
        )

    y_copies = [[], []]
    for a in range(2):
        loads[a].wait()
        if a == 1:
            for c in loads[2:]:
                c.start()
        for h in range(2):
            pick(a, h)
            if a == 0 and h == 0:
                pl.semaphore_wait(barrier, len(plane) + n_out - 1)
            for d in range(1, n_out):
                c = y_copy(a, h, d)
                c.start()
                y_copies[a].append(c)

    row = lax.broadcasted_iota(jnp.int32, (slots, cols), 0)
    pcol = lax.broadcasted_iota(jnp.int32, (slots, cols), 1)
    compact = jnp.where((row // CAP) * PAD + lax.rem(row, CAP) == pcol, 1.0, 0.0).astype(BF)

    def gather_own(a, h):
        own = pl.ds(h * half, half)
        for d in range(1, n_out):
            pltpu.make_async_remote_copy(
                src_ref=ysend.at[a, 0, :, own],
                dst_ref=yrecv.at[a, lax.rem(me_o + n_out - d, n_out), :, own],
                send_sem=y_send_sem.at[a, h, d],
                recv_sem=y_recv_sem.at[a, h, d],
                device_id=(peer(d), me_i),
                device_id_type=MESH,
            ).wait_recv()

        def step(j, carry):
            s = part_span(h * half, j)
            v = yrecv[a, :, :, s].reshape(cols, eighth)
            rows[a, me_i, :, s] = dot(compact, v, NN).astype(BF)
            return carry

        lax.fori_loop(0, 4, step, 0)

    started = []

    def piece(a, f, s, h):
        ref = rows.at[a, block(a, f, s)]
        return ref if h is None else ref.at[:, pl.ds(h * half, half)]

    def ag(a, k, f, s, h, f_to, s_to):
        c = pltpu.make_async_remote_copy(
            src_ref=piece(a, f, s, h),
            dst_ref=piece(a, f, s, h),
            send_sem=ag_send.at[a, k, h or 0],
            recv_sem=ag_recv.at[a, k, h or 0],
            device_id=(me_o, block(a, f_to, s_to)),
            device_id_type=MESH,
        )
        c.start()
        started.append(c)

    def ag_wait(a, k, f, s, h):
        pltpu.make_async_remote_copy(
            src_ref=piece(a, f, s, h),
            dst_ref=piece(a, f, s, h),
            send_sem=ag_send.at[a, k, h or 0],
            recv_sem=ag_recv.at[a, k, h or 0],
            device_id=(me_o, block(a, first[a], second[a])),
            device_id_type=MESH,
        ).wait_recv()

    def out_second(a, off):
        f, s = first[a], second[a]
        ag(a, 4 + off, ring(f, off), s, None, f, ring(s, 1))
        ag(a, 8 + off, ring(f, off), s, None, f, ring(s, 3))

    def on_second_plus(a, off):
        f, s = ring(first[a], off), second[a]
        for h in (0, 1) if off == 0 else (None,):
            ag_wait(a, 4 + off, f, ring(s, 3), h)
        ag(a, 12 + off, f, ring(s, 3), 0, first[a], ring(s, 1))

    def on_second_minus(a, off):
        f, s = ring(first[a], off), second[a]
        for h in (0, 1) if off == 0 else (None,):
            ag_wait(a, 8 + off, f, ring(s, 1), h)
        ag(a, 16 + off, f, ring(s, 1), 1, first[a], ring(s, 3))

    def on_second_far(a, off):
        f, s = ring(first[a], off), second[a]
        ag_wait(a, 12 + off, f, ring(s, 2), 0)
        ag_wait(a, 16 + off, f, ring(s, 2), 1)

    def round0(a, h):
        f, s = first[a], second[a]
        ag(a, 0, f, s, h, ring(f, 1), s)
        ag(a, 1, f, s, h, ring(f, 3), s)
        ag(a, 4, f, s, h, f, ring(s, 1))
        ag(a, 8, f, s, h, f, ring(s, 3))

    def round1(a):
        f, s = first[a], second[a]
        ag_wait(a, 0, ring(f, 3), s, 0)
        ag(a, 2, ring(f, 3), s, 0, ring(f, 1), s)
        ag_wait(a, 0, ring(f, 3), s, 1)
        out_second(a, 3)
        ag_wait(a, 1, ring(f, 1), s, 0)
        ag_wait(a, 1, ring(f, 1), s, 1)
        ag(a, 3, ring(f, 1), s, 1, ring(f, 3), s)
        out_second(a, 1)
        on_second_plus(a, 0)
        on_second_minus(a, 0)

    def round2(a):
        f, s = first[a], second[a]
        ag_wait(a, 2, ring(f, 2), s, 0)
        ag_wait(a, 3, ring(f, 2), s, 1)
        out_second(a, 2)

    def round2_on(a):
        for off in (3, 1):
            on_second_plus(a, off)
            on_second_minus(a, off)

    def round3(a):
        on_second_plus(a, 2)
        on_second_minus(a, 2)

    def forward(a, blocks):
        for off_f, off_s in blocks:
            b = block(a, ring(first[a], off_f), ring(second[a], off_s))
            if a == 0:

                def step(j, acc, b=b):
                    return acc + dot(rows[0, b, :, span(j)], wgu[span(j), :], NN)

                gu[b] = lax.fori_loop(0, n_c, step, jnp.zeros((slots, 256), F32))
            else:

                def step(j, acc, b=b):
                    return acc + dot(rows[1, b, :, span(j)], wd[:, span(j)], NT)

                hid[b] = lax.fori_loop(0, n_c, step, jnp.zeros((slots, 128), F32))

    for a in range(2):
        for h in range(2):
            gather_own(a, h)
            round0(a, h)
    for c in loads[2:]:
        c.wait()
    for a in range(2):
        forward(a, [(0, 0)])
    round1(0)
    round1(1)
    for a in range(2):
        forward(a, [(1, 0), (3, 0), (0, 1), (0, 3)])
    round2(0)
    round2(1)
    round2_on(0)
    round2_on(1)
    for a in range(2):
        on_second_far(a, 0)
        forward(a, [(2, 0), (1, 1), (3, 1), (1, 3), (3, 3), (0, 2)])
    round3(0)
    round3(1)
    for a in range(2):
        on_second_far(a, 1)
        on_second_far(a, 3)
        forward(a, [(2, 1), (2, 3), (1, 2), (3, 2)])
    def nonlinear(b, carry):
        gate = gu[b, :, 0:128]
        up = gu[b, :, 128:256]
        grad = hid[b]
        sig = jax.nn.sigmoid(gate)
        silu = gate * sig
        act[b] = (silu * up).astype(BF)
        ggug[b, :, 0:128] = (grad * up * sig * (1.0 + gate * (1.0 - sig))).astype(BF)
        ggug[b, :, 128:256] = (grad * silu).astype(BF)
        return carry

    last = ring(my_z, 2) * SIDE + ring(my_x, 2)

    def nonlinear_early(j, carry):
        return nonlinear(lax.rem(last + j, SIDE * SIDE), carry)

    lax.fori_loop(1, SIDE * SIDE, nonlinear_early, 0)

    p_of = (my_z, my_x)
    q_of = (my_x, my_z)

    def rs_block(a, p, q):
        return p * SIDE + q if a == 0 else q * SIDE + p

    def rs_dev(a, p, q):
        return (me_o, rs_block(a, p, q))

    def rs_copy(a, c, k, src, dst, p, q):
        return pltpu.make_async_remote_copy(
            src_ref=src,
            dst_ref=dst,
            send_sem=rs_send.at[a, c, k],
            recv_sem=rs_recv.at[a, c, k],
            device_id=rs_dev(a, p, q),
            device_id_type=MESH,
        )

    def terms(a, c, p, qs, put):
        m = jnp.concatenate([ggug[rs_block(a, p, q)] for q in qs], axis=0)

        def step(j, carry):
            w = wgu[part_span(a * half + c * quarter, j), :]
            v = dot(m, w, NT).reshape(len(qs), slots, eighth)
            put(v, part_span(c * quarter, j))
            return carry

        lax.fori_loop(0, 2, step, 0)

    lo, hi = pl.ds(0, 2), pl.ds(2, 2)

    def phase_copies(a, c):
        p, q = p_of[a], q_of[a]
        up, dn = (ring(p, 1), q), (ring(p, 3), q)
        qu, qd = (p, ring(q, 1)), (p, ring(q, 3))
        cc = pl.ds(c * quarter, quarter)
        c0, c1 = pl.ds(c * quarter, eighth), pl.ds(c * quarter + eighth, eighth)
        ce = pl.ds(c * eighth, eighth)
        far, nxt, prv = part.at[a, ring(q, 2)], part.at[a, ring(q, 1)], part.at[a, ring(q, 3)]
        return [
            rs_copy(a, c, 0, sf.at[a, 0, :, :, cc], rf.at[a, 0, :, :, cc], *up),
            rs_copy(a, c, 1, sf.at[a, 1, :, :, cc], rf.at[a, 1, :, :, cc], *dn),
            rs_copy(a, c, 2, sn.at[a, 0, hi, :, cc], rn.at[a, 0, hi, :, cc], *up),
            rs_copy(a, c, 3, sn.at[a, 1, lo, :, cc], rn.at[a, 1, lo, :, cc], *dn),
            rs_copy(a, c, 4, sn.at[a, 0, lo, :, cc], rn.at[a, 0, lo, :, cc], *up),
            rs_copy(a, c, 5, sn.at[a, 1, hi, :, cc], rn.at[a, 1, hi, :, cc], *dn),
            rs_copy(a, c, 6, far.at[:, c0], rf2.at[a, 0, :, ce], *qu),
            rs_copy(a, c, 7, far.at[:, c1], rf2.at[a, 1, :, ce], *qd),
            rs_copy(a, c, 8, nxt.at[:, c1], rn2.at[a, 0, :, c1], *qu),
            rs_copy(a, c, 9, prv.at[:, c0], rn2.at[a, 1, :, c0], *qd),
            rs_copy(a, c, 10, nxt.at[:, c0], rn2.at[a, 0, :, c0], *qu),
            rs_copy(a, c, 11, prv.at[:, c1], rn2.at[a, 1, :, c1], *qd),
        ]

    rs = [[phase_copies(a, c) for c in range(2)] for a in range(2)]

    def near_at_once(a, c):
        def put_up(v, s):
            sn[a, 0, 2:4, :, s] = v.astype(BF)

        def put_dn(v, s):
            sn[a, 1, 0:2, :, s] = v.astype(BF)

        terms(a, c, ring(p_of[a], 1), (2, 3), put_up)
        rs[a][c][2].start()
        terms(a, c, ring(p_of[a], 3), (0, 1), put_dn)
        rs[a][c][3].start()

    def far_part(a, c):
        def put_far(v, s):
            sf[a, 0, :, :, s] = v[0:2].astype(BF)
            sf[a, 1, :, :, s] = v[2:4].astype(BF)

        terms(a, c, ring(p_of[a], 2), (0, 1, 2, 3), put_far)
        rs[a][c][0].start()
        rs[a][c][1].start()

    def near_after(a, c):
        def put_up2(v, s):
            sn[a, 0, 0:2, :, s] = (v + rf[a, 0, :, :, s].astype(F32)).astype(BF)

        def put_dn2(v, s):
            sn[a, 1, 2:4, :, s] = (v + rf[a, 1, :, :, s].astype(F32)).astype(BF)

        rs[a][c][0].wait_recv()
        terms(a, c, ring(p_of[a], 1), (0, 1), put_up2)
        rs[a][c][4].start()
        rs[a][c][1].wait_recv()
        terms(a, c, ring(p_of[a], 3), (2, 3), put_dn2)
        rs[a][c][5].start()

    for a in range(2):
        near_at_once(a, 0)
    for a in range(2):
        on_second_far(a, 2)
        forward(a, [(2, 2)])
    nonlinear(last, 0)
    for c in range(2):
        for a in range(2):
            far_part(a, c)
    for a in range(2):
        near_at_once(a, 1)

    gw = 512

    def grad_step(j, carry):
        slot = lax.rem(j, 2)

        def outs(i):
            dst = pl.ds(pl.multiple_of(i * gw, gw), gw)
            return (
                pltpu.make_async_copy(
                    stage.at[slot, :, pl.ds(0, 128)], gate_hbm.at[dst, :], out_sem.at[0, slot]
                ),
                pltpu.make_async_copy(
                    stage.at[slot, :, pl.ds(128, 128)], up_hbm.at[dst, :], out_sem.at[1, slot]
                ),
            )

        @pl.when(j >= 2)
        def _():
            for c in outs(j - 2):
                c.wait()

        xs = rows[0, :, :, span(j, gw)].reshape(SIDE * SIDE * slots, gw)
        stage[slot] = dot(xs, ggug[...].reshape(SIDE * SIDE * slots, 256), TN)
        for c in outs(j):
            c.start()
        return carry

    def down_step(j, carry):
        slot = lax.rem(j, 2)

        def out(i):
            return pltpu.make_async_copy(
                stage_d.at[slot], down_hbm.at[:, span(i, gw)], out_d_sem.at[slot]
            )

        @pl.when(j >= 2)
        def _():
            out(j - 2).wait()

        gs = rows[1, :, :, span(j, gw)].reshape(SIDE * SIDE * slots, gw)
        stage_d[slot] = dot(act[...].reshape(SIDE * SIDE * slots, 128), gs, TN)
        out(j).start()
        return carry

    n_g = width // gw
    lax.fori_loop(0, n_g, down_step, 0)
    for c in range(2):
        for a in range(2):
            near_after(a, c)
    lax.fori_loop(0, n_g, grad_step, 0)

    for c in range(2):
        for a in range(2):
            for k in (2, 3, 4, 5):
                rs[a][c][k].wait_recv()

            def put_part(v, s, a=a):
                t = v + rn[a, 0, :, :, s].astype(F32) + rn[a, 1, :, :, s].astype(F32)
                part[a, :, :, s] = t.astype(BF)

            terms(a, c, p_of[a], (0, 1, 2, 3), put_part)
            for k in (6, 7, 8, 9):
                rs[a][c][k].start()
    for c in range(2):
        ce = pl.ds(c * eighth, eighth)
        for a in range(2):
            for k, off, col0, r in ((6, 1, 0, 0), (7, 3, eighth, 1)):
                rs[a][c][k].wait_recv()
                b = ring(q_of[a], off)
                s = pl.ds(c * quarter + col0, eighth)
                t = part[a, b, :, s].astype(F32) + rf2[a, r, :, ce].astype(F32)
                part[a, b, :, s] = t.astype(BF)
                rs[a][c][k + 4].start()

    for c in y_copies[0]:
        c.wait_send()
    spread = jnp.where(
        (lax.broadcasted_iota(jnp.int32, (cols, slots), 1) // CAP) * PAD
        + lax.rem(lax.broadcasted_iota(jnp.int32, (cols, slots), 1), CAP)
        == lax.broadcasted_iota(jnp.int32, (cols, slots), 0),
        1.0,
        0.0,
    ).astype(BF)
    back_copies = []
    for c in range(2):
        for a in range(2):
            for k in (8, 9, 10, 11):
                rs[a][c][k].wait_recv()
            first_col = a * half + c * quarter

            def final_step(j, carry, a=a, c=c, first_col=first_col):
                s = part_span(c * quarter, j)
                t = part[a, q_of[a], :, s].astype(F32) + rn2[a, 0, :, s].astype(F32)
                t = (t + rn2[a, 1, :, s].astype(F32)).astype(BF)
                v = dot(spread, t, NN).astype(BF).reshape(n_out, PAD, eighth)
                ysend[0, :, :, part_span(first_col, j)] = v
                return carry

            lax.fori_loop(0, 2, final_step, 0)
            seg = pl.ds(first_col, quarter)
            for d in range(1, n_out):
                copy = pltpu.make_async_remote_copy(
                    src_ref=ysend.at[0, peer(d), :, seg],
                    dst_ref=back.at[me_o, :, seg],
                    send_sem=b_send_sem.at[a, c, d],
                    recv_sem=b_recv_sem.at[a, c, d],
                    device_id=(peer(d), me_i),
                    device_id_type=MESH,
                )
                copy.start()
                back_copies.append(copy)
            back[me_o, :, seg] = ysend[0, me_o, :, seg]
    back_outs = []
    for c in range(2):
        for a in range(2):
            seg = pl.ds(a * half + c * quarter, quarter)
            for d in range(1, n_out):
                pltpu.make_async_remote_copy(
                    src_ref=ysend.at[0, 0, :, seg],
                    dst_ref=back.at[lax.rem(me_o + n_out - d, n_out), :, seg],
                    send_sem=b_send_sem.at[a, c, d],
                    recv_sem=b_recv_sem.at[a, c, d],
                    device_id=(peer(d), me_i),
                    device_id_type=MESH,
                ).wait_recv()
            copy = pltpu.make_async_copy(
                back.at[:, :, seg], back_hbm.at[:, :, seg], b_out_sem.at[a, c]
            )
            copy.start()
            back_outs.append(copy)

    for c in started:
        c.wait_send()
    for c in y_copies[1]:
        c.wait_send()
    for c in back_copies:
        c.wait_send()
    for a in range(2):
        for chunk in rs[a]:
            for c in chunk:
                c.wait_send()
    for i in (n_g - 2, n_g - 1):
        slot = i % 2
        dst = pl.ds(i * gw, gw)
        pltpu.make_async_copy(
            stage.at[slot, :, pl.ds(0, 128)], gate_hbm.at[dst, :], out_sem.at[0, slot]
        ).wait()
        pltpu.make_async_copy(
            stage.at[slot, :, pl.ds(128, 128)], up_hbm.at[dst, :], out_sem.at[1, slot]
        ).wait()
        pltpu.make_async_copy(
            stage_d.at[slot], down_hbm.at[:, dst], out_d_sem.at[slot]
        ).wait()
    for c in back_outs:
        c.wait()
    place_out.wait()


def shards(layer_input, out_grad, expert_ids, route_scales, w_gate, w_up, w_down):
    toks, width = layer_input.shape
    n_out = lax.axis_size("outer")
    n_in = lax.axis_size("inner")
    hidden = w_gate.shape[2]
    slots = n_out * CAP
    half, quarter = width // 2, width // 4
    any_spec = pl.BlockSpec(memory_space=pl.ANY)
    vmem = pl.BlockSpec(memory_space=pltpu.VMEM)
    dma = pltpu.SemaphoreType.DMA
    back, place, gate, up, down = pl.pallas_call(
        kernel,
        out_shape=(
            jax.ShapeDtypeStruct((n_out, PAD, width), BF),
            jax.ShapeDtypeStruct((toks, n_out * PAD), BF),
            jax.ShapeDtypeStruct((width, hidden), F32),
            jax.ShapeDtypeStruct((width, hidden), F32),
            jax.ShapeDtypeStruct((hidden, width), F32),
        ),
        in_specs=[vmem, vmem] + [any_spec] * 5,
        out_specs=(any_spec,) * 5,
        scratch_shapes=[
            pltpu.VMEM((2, toks, width), BF),
            pltpu.VMEM((width, 2 * hidden), BF),
            pltpu.VMEM((hidden, width), BF),
            pltpu.VMEM((toks, n_out * PAD), BF),
            pltpu.VMEM((2, n_out, PAD, width), BF),
            pltpu.VMEM((2, n_out, PAD, width), BF),
            pltpu.VMEM((n_out, PAD, width), BF),
            pltpu.VMEM((2, n_in, slots, width), BF),
            pltpu.VMEM((n_in, slots, 2 * hidden), F32),
            pltpu.VMEM((n_in, slots, hidden), F32),
            pltpu.VMEM((n_in, slots, 2 * hidden), BF),
            pltpu.VMEM((n_in, slots, hidden), BF),
            pltpu.VMEM((2, 2, 2, slots, half), BF),
            pltpu.VMEM((2, 2, 2, slots, half), BF),
            pltpu.VMEM((2, 2, SIDE, slots, half), BF),
            pltpu.VMEM((2, 2, SIDE, slots, half), BF),
            pltpu.VMEM((2, SIDE, slots, half), BF),
            pltpu.VMEM((2, 2, slots, quarter), BF),
            pltpu.VMEM((2, 2, slots, half), BF),
            pltpu.VMEM((2, 512, 2 * hidden), F32),
            pltpu.VMEM((2, hidden, 512), F32),
            dma((5,)),
            dma((2, 2, n_out)),
            dma((2, 2, n_out)),
            dma((2, 2, n_out)),
            dma((2, 2, n_out)),
            dma((2, 20, 2)),
            dma((2, 20, 2)),
            dma((2, 2, 12)),
            dma((2, 2, 12)),
            dma((2, 2)),
            dma((2,)),
            dma((2, 2)),
            dma,
        ],
        compiler_params=pltpu.CompilerParams(
            collective_id=0, has_side_effects=True, vmem_limit_bytes=67043328
        ),
        name="expert_backward",
    )(expert_ids.T, route_scales.T, layer_input, out_grad, w_gate[0], w_up[0], w_down[0])
    in_grad = dot(place, back.reshape(n_out * PAD, width), NN).astype(BF)
    return in_grad, gate[None], up[None], down[None]


def solution(mesh):
    return jax.shard_map(
        shards,
        mesh=mesh,
        in_specs=(
            P(("outer", "inner"), None),
            P(("outer", "inner"), None),
            P(("outer", "inner"), None),
            P(("outer", "inner"), None),
            P("outer", None, "inner"),
            P("outer", None, "inner"),
            P("outer", "inner", None),
        ),
        out_specs=(
            P(("outer", "inner"), None),
            P("outer", None, "inner"),
            P("outer", None, "inner"),
            P("outer", "inner", None),
        ),
        check_vma=False,
    )
```

```python
import jax
import jax.numpy as jnp
from jax import lax
from jax.experimental import pallas as pl
from jax.experimental.pallas import tpu as pltpu
from jax.sharding import PartitionSpec as P

CAP = 6
PAD = 8
SIDE = 4
BF = jnp.bfloat16
F32 = jnp.float32
MESH = pl.DeviceIdType.MESH
NN = (((1,), (0,)), ((), ()))
NT = (((1,), (1,)), ((), ()))
TN = (((0,), (0,)), ((), ()))


def dot(a, b, dims):
    return lax.dot_general(a, b, dims, preferred_element_type=F32)


def kernel(
    ids_ref, scale_ref, x_hbm, dy_hbm, wg_hbm, wu_hbm, wd_hbm,
    back_hbm, place_hbm, gate_hbm, up_hbm, down_hbm,
    tok, wgu, wd, place, ysend, yrecv, back, rows, gu, hid, ggug, act,
    sf, rf, sn, rn, part, rf2, rn2, stage, stage_d,
    load_sem, y_send_sem, y_recv_sem, b_send_sem, b_recv_sem,
    ag_send, ag_recv, rs_send, rs_recv, out_sem, out_d_sem, b_out_sem, place_sem,
):
    n_out = ysend.shape[1]
    width = tok.shape[2]
    half = width // 2
    quarter = width // 4
    eighth = width // 8
    slots = n_out * CAP
    me_o = lax.axis_index("outer")
    me_i = lax.axis_index("inner")
    my_z = me_i // SIDE
    my_x = lax.rem(me_i, SIDE)

    def ring(v, k):
        return lax.rem(v + k, SIDE)

    def peer(d):
        return lax.rem(me_o + d, n_out)

    first = (my_x, my_z)
    second = (my_z, my_x)

    def block(a, f, s):
        return s * SIDE + f if a == 0 else f * SIDE + s

    barrier = pltpu.get_barrier_semaphore()
    plane = [
        my_z * SIDE + ring(my_x, 1), my_z * SIDE + ring(my_x, 3),
        ring(my_z, 1) * SIDE + my_x, ring(my_z, 3) * SIDE + my_x,
    ]
    for i in plane:
        pl.semaphore_signal(barrier, inc=1, device_id=(me_o, i), device_id_type=MESH)
    for d in range(1, n_out):
        pl.semaphore_signal(barrier, inc=1, device_id=(peer(d), me_i), device_id_type=MESH)

    loads = [
        pltpu.make_async_copy(x_hbm, tok.at[0], load_sem.at[0]),
        pltpu.make_async_copy(dy_hbm, tok.at[1], load_sem.at[1]),
        pltpu.make_async_copy(wg_hbm, wgu.at[:, pl.ds(0, 128)], load_sem.at[2]),
        pltpu.make_async_copy(wu_hbm, wgu.at[:, pl.ds(128, 128)], load_sem.at[3]),
        pltpu.make_async_copy(wd_hbm, wd, load_sem.at[4]),
    ]
    for c in loads[:2]:
        c.start()

    ids = jnp.transpose(ids_ref[...].astype(F32))
    scales = jnp.transpose(scale_ref[...])
    toks = ids.shape[0]
    cols = n_out * PAD
    col = lax.broadcasted_iota(jnp.int32, (toks, cols), 1)
    col_expert = (col // PAD).astype(F32)
    col_slot = lax.rem(col, PAD)
    named = jnp.zeros((toks, cols), F32)
    weight = jnp.zeros((toks, cols), F32)
    for k in range(ids.shape[1]):
        hit = ids[:, k : k + 1] == col_expert
        named = named + jnp.where(hit, 1.0, 0.0)
        weight = weight + jnp.where(hit, scales[:, k : k + 1], 0.0)
    earlier = jnp.where(
        lax.broadcasted_iota(jnp.int32, (toks, toks), 0)
        > lax.broadcasted_iota(jnp.int32, (toks, toks), 1),
        1.0,
        0.0,
    ).astype(BF)
    position = dot(earlier, named.astype(BF), NN)
    chosen = jnp.where(position == col_slot.astype(F32), named, 0.0)
    place[...] = chosen.astype(BF)
    place_out = pltpu.make_async_copy(place, place_hbm, place_sem)
    place_out.start()
    slot_scale = jnp.sum(jnp.transpose(chosen * weight), axis=1, keepdims=True)
    place_t = jnp.transpose(chosen).astype(BF)

    cw = 1024
    n_c = width // cw

    def span(j, w=cw):
        return pl.ds(pl.multiple_of(j * w, w), w)

    def part_span(first_col, j):
        return pl.ds(pl.multiple_of(first_col + j * eighth, eighth), eighth)

    def pick(a, h):
        def step(j, carry):
            s = part_span(h * half, j)
            v = dot(place_t, tok[a, :, s], NN)
            if a == 1:
                v = v * slot_scale
            ysend[a, :, :, s] = v.astype(BF).reshape(n_out, PAD, eighth)
            return carry

        lax.fori_loop(0, 4, step, 0)
        own = pl.ds(h * half, half)
        yrecv[a, me_o, :, own] = ysend[a, me_o, :, own]

    def y_copy(a, h, d):
        own = pl.ds(h * half, half)
        return pltpu.make_async_remote_copy(
            src_ref=ysend.at[a, peer(d), :, own],
            dst_ref=yrecv.at[a, me_o, :, own],
            send_sem=y_send_sem.at[a, h, d],
            recv_sem=y_recv_sem.at[a, h, d],
            device_id=(peer(d), me_i),
            device_id_type=MESH,
        )

    y_copies = [[], []]
    for a in range(2):
        loads[a].wait()
        if a == 1:
            for c in loads[2:]:
                c.start()
        for h in range(2):
            pick(a, h)
            if a == 0 and h == 0:
                pl.semaphore_wait(barrier, len(plane) + n_out - 1)
            for d in range(1, n_out):
                c = y_copy(a, h, d)
                c.start()
                y_copies[a].append(c)

    row = lax.broadcasted_iota(jnp.int32, (slots, cols), 0)
    pcol = lax.broadcasted_iota(jnp.int32, (slots, cols), 1)
    compact = jnp.where((row // CAP) * PAD + lax.rem(row, CAP) == pcol, 1.0, 0.0).astype(BF)

    def gather_own(a, h):
        own = pl.ds(h * half, half)
        for d in range(1, n_out):
            pltpu.make_async_remote_copy(
                src_ref=ysend.at[a, 0, :, own],
                dst_ref=yrecv.at[a, lax.rem(me_o + n_out - d, n_out), :, own],
                send_sem=y_send_sem.at[a, h, d],
                recv_sem=y_recv_sem.at[a, h, d],
                device_id=(peer(d), me_i),
                device_id_type=MESH,
            ).wait_recv()

        def step(j, carry):
            s = part_span(h * half, j)
            v = yrecv[a, :, :, s].reshape(cols, eighth)
            rows[a, me_i, :, s] = dot(compact, v, NN).astype(BF)
            return carry

        lax.fori_loop(0, 4, step, 0)

    started = []

    def piece(a, f, s, h):
        ref = rows.at[a, block(a, f, s)]
        return ref if h is None else ref.at[:, pl.ds(h * half, half)]

    def ag(a, k, f, s, h, f_to, s_to):
        c = pltpu.make_async_remote_copy(
            src_ref=piece(a, f, s, h),
            dst_ref=piece(a, f, s, h),
            send_sem=ag_send.at[a, k, h or 0],
            recv_sem=ag_recv.at[a, k, h or 0],
            device_id=(me_o, block(a, f_to, s_to)),
            device_id_type=MESH,
        )
        c.start()
        started.append(c)

    def ag_wait(a, k, f, s, h):
        pltpu.make_async_remote_copy(
            src_ref=piece(a, f, s, h),
            dst_ref=piece(a, f, s, h),
            send_sem=ag_send.at[a, k, h or 0],
            recv_sem=ag_recv.at[a, k, h or 0],
            device_id=(me_o, block(a, first[a], second[a])),
            device_id_type=MESH,
        ).wait_recv()

    def out_second(a, off):
        f, s = first[a], second[a]
        ag(a, 4 + off, ring(f, off), s, None, f, ring(s, 1))
        ag(a, 8 + off, ring(f, off), s, None, f, ring(s, 3))

    def on_second_plus(a, off):
        f, s = ring(first[a], off), second[a]
        for h in (0, 1) if off == 0 else (None,):
            ag_wait(a, 4 + off, f, ring(s, 3), h)
        ag(a, 12 + off, f, ring(s, 3), 0, first[a], ring(s, 1))

    def on_second_minus(a, off):
        f, s = ring(first[a], off), second[a]
        for h in (0, 1) if off == 0 else (None,):
            ag_wait(a, 8 + off, f, ring(s, 1), h)
        ag(a, 16 + off, f, ring(s, 1), 1, first[a], ring(s, 3))

    def on_second_far(a, off):
        f, s = ring(first[a], off), second[a]
        ag_wait(a, 12 + off, f, ring(s, 2), 0)
        ag_wait(a, 16 + off, f, ring(s, 2), 1)

    def round0(a, h):
        f, s = first[a], second[a]
        ag(a, 0, f, s, h, ring(f, 1), s)
        ag(a, 1, f, s, h, ring(f, 3), s)
        ag(a, 4, f, s, h, f, ring(s, 1))
        ag(a, 8, f, s, h, f, ring(s, 3))

    def round1(a):
        f, s = first[a], second[a]
        ag_wait(a, 0, ring(f, 3), s, 0)
        ag(a, 2, ring(f, 3), s, 0, ring(f, 1), s)
        ag_wait(a, 0, ring(f, 3), s, 1)
        out_second(a, 3)
        ag_wait(a, 1, ring(f, 1), s, 0)
        ag_wait(a, 1, ring(f, 1), s, 1)
        ag(a, 3, ring(f, 1), s, 1, ring(f, 3), s)
        out_second(a, 1)
        on_second_plus(a, 0)
        on_second_minus(a, 0)

    def round2(a):
        f, s = first[a], second[a]
        ag_wait(a, 2, ring(f, 2), s, 0)
        ag_wait(a, 3, ring(f, 2), s, 1)
        out_second(a, 2)

    def round2_on(a):
        for off in (3, 1):
            on_second_plus(a, off)
            on_second_minus(a, off)

    def round3(a):
        on_second_plus(a, 2)
        on_second_minus(a, 2)

    def forward(a, blocks):
        size = 3 if len(blocks) == 6 else 4
        for start in range(0, len(blocks), size):
            bs = [
                block(a, ring(first[a], off_f), ring(second[a], off_s))
                for off_f, off_s in blocks[start : start + size]
            ]

            def step(j, acc, bs=bs):
                m = jnp.concatenate([rows[a, b, :, span(j)] for b in bs], axis=0)
                if a == 0:
                    return acc + dot(m, wgu[span(j), :], NN)
                return acc + dot(m, wd[:, span(j)], NT)

            out = gu if a == 0 else hid
            acc = jnp.zeros((len(bs) * slots, out.shape[2]), F32)
            acc = lax.fori_loop(0, n_c, step, acc)
            for n, b in enumerate(bs):
                out[b] = acc[n * slots : (n + 1) * slots]

    for a in range(2):
        for h in range(2):
            gather_own(a, h)
            round0(a, h)
    for c in loads[2:]:
        c.wait()
    for a in range(2):
        forward(a, [(0, 0)])
    round1(0)
    round1(1)
    for a in range(2):
        forward(a, [(1, 0), (3, 0), (0, 1), (0, 3)])
    round2(0)
    round2(1)
    round2_on(0)
    round2_on(1)
    for a in range(2):
        on_second_far(a, 0)
        forward(a, [(2, 0), (1, 1), (3, 1), (1, 3), (3, 3), (0, 2)])
    round3(0)
    round3(1)
    for a in range(2):
        on_second_far(a, 1)
        on_second_far(a, 3)
        forward(a, [(2, 1), (2, 3), (1, 2), (3, 2)])
    def nonlinear(b, carry):
        gate = gu[b, :, 0:128]
        up = gu[b, :, 128:256]
        grad = hid[b]
        sig = jax.nn.sigmoid(gate)
        silu = gate * sig
        act[b] = (silu * up).astype(BF)
        ggug[b, :, 0:128] = (grad * up * sig * (1.0 + gate * (1.0 - sig))).astype(BF)
        ggug[b, :, 128:256] = (grad * silu).astype(BF)
        return carry

    last = ring(my_z, 2) * SIDE + ring(my_x, 2)

    def nonlinear_early(j, carry):
        return nonlinear(lax.rem(last + j, SIDE * SIDE), carry)

    lax.fori_loop(1, SIDE * SIDE, nonlinear_early, 0)

    p_of = (my_z, my_x)
    q_of = (my_x, my_z)

    def rs_block(a, p, q):
        return p * SIDE + q if a == 0 else q * SIDE + p

    def rs_dev(a, p, q):
        return (me_o, rs_block(a, p, q))

    def rs_copy(a, c, k, src, dst, p, q):
        return pltpu.make_async_remote_copy(
            src_ref=src,
            dst_ref=dst,
            send_sem=rs_send.at[a, c, k],
            recv_sem=rs_recv.at[a, c, k],
            device_id=rs_dev(a, p, q),
            device_id_type=MESH,
        )

    def terms(a, c, p, qs, put):
        m = jnp.concatenate([ggug[rs_block(a, p, q)] for q in qs], axis=0)

        def step(j, carry):
            w = wgu[part_span(a * half + c * quarter, j), :]
            v = dot(m, w, NT).reshape(len(qs), slots, eighth)
            put(v, part_span(c * quarter, j))
            return carry

        lax.fori_loop(0, 2, step, 0)

    lo, hi = pl.ds(0, 2), pl.ds(2, 2)

    def phase_copies(a, c):
        p, q = p_of[a], q_of[a]
        up, dn = (ring(p, 1), q), (ring(p, 3), q)
        qu, qd = (p, ring(q, 1)), (p, ring(q, 3))
        cc = pl.ds(c * quarter, quarter)
        c0, c1 = pl.ds(c * quarter, eighth), pl.ds(c * quarter + eighth, eighth)
        ce = pl.ds(c * eighth, eighth)
        far, nxt, prv = part.at[a, ring(q, 2)], part.at[a, ring(q, 1)], part.at[a, ring(q, 3)]
        return [
            rs_copy(a, c, 0, sf.at[a, 0, :, :, cc], rf.at[a, 0, :, :, cc], *up),
            rs_copy(a, c, 1, sf.at[a, 1, :, :, cc], rf.at[a, 1, :, :, cc], *dn),
            rs_copy(a, c, 2, sn.at[a, 0, hi, :, cc], rn.at[a, 0, hi, :, cc], *up),
            rs_copy(a, c, 3, sn.at[a, 1, lo, :, cc], rn.at[a, 1, lo, :, cc], *dn),
            rs_copy(a, c, 4, sn.at[a, 0, lo, :, cc], rn.at[a, 0, lo, :, cc], *up),
            rs_copy(a, c, 5, sn.at[a, 1, hi, :, cc], rn.at[a, 1, hi, :, cc], *dn),
            rs_copy(a, c, 6, far.at[:, c0], rf2.at[a, 0, :, ce], *qu),
            rs_copy(a, c, 7, far.at[:, c1], rf2.at[a, 1, :, ce], *qd),
            rs_copy(a, c, 8, nxt.at[:, c1], rn2.at[a, 0, :, c1], *qu),
            rs_copy(a, c, 9, prv.at[:, c0], rn2.at[a, 1, :, c0], *qd),
            rs_copy(a, c, 10, nxt.at[:, c0], rn2.at[a, 0, :, c0], *qu),
            rs_copy(a, c, 11, prv.at[:, c1], rn2.at[a, 1, :, c1], *qd),
        ]

    rs = [[phase_copies(a, c) for c in range(2)] for a in range(2)]

    def near_at_once(a, c):
        def put_up(v, s):
            sn[a, 0, 2:4, :, s] = v.astype(BF)

        def put_dn(v, s):
            sn[a, 1, 0:2, :, s] = v.astype(BF)

        terms(a, c, ring(p_of[a], 1), (2, 3), put_up)
        rs[a][c][2].start()
        terms(a, c, ring(p_of[a], 3), (0, 1), put_dn)
        rs[a][c][3].start()

    def far_part(a, c):
        def put_far(v, s):
            sf[a, 0, :, :, s] = v[0:2].astype(BF)
            sf[a, 1, :, :, s] = v[2:4].astype(BF)

        terms(a, c, ring(p_of[a], 2), (0, 1, 2, 3), put_far)
        rs[a][c][0].start()
        rs[a][c][1].start()

    def near_after(a, c):
        def put_up2(v, s):
            sn[a, 0, 0:2, :, s] = (v + rf[a, 0, :, :, s].astype(F32)).astype(BF)

        def put_dn2(v, s):
            sn[a, 1, 2:4, :, s] = (v + rf[a, 1, :, :, s].astype(F32)).astype(BF)

        rs[a][c][0].wait_recv()
        terms(a, c, ring(p_of[a], 1), (0, 1), put_up2)
        rs[a][c][4].start()
        rs[a][c][1].wait_recv()
        terms(a, c, ring(p_of[a], 3), (2, 3), put_dn2)
        rs[a][c][5].start()

    for a in range(2):
        near_at_once(a, 0)
    for a in range(2):
        on_second_far(a, 2)
        forward(a, [(2, 2)])
    nonlinear(last, 0)
    for c in range(2):
        for a in range(2):
            far_part(a, c)
    for a in range(2):
        near_at_once(a, 1)

    gw = 512

    def grad_step(j, carry):
        slot = lax.rem(j, 2)

        def outs(i):
            dst = pl.ds(pl.multiple_of(i * gw, gw), gw)
            return (
                pltpu.make_async_copy(
                    stage.at[slot, :, pl.ds(0, 128)], gate_hbm.at[dst, :], out_sem.at[0, slot]
                ),
                pltpu.make_async_copy(
                    stage.at[slot, :, pl.ds(128, 128)], up_hbm.at[dst, :], out_sem.at[1, slot]
                ),
            )

        @pl.when(j >= 2)
        def _():
            for c in outs(j - 2):
                c.wait()

        xs = rows[0, :, :, span(j, gw)].reshape(SIDE * SIDE * slots, gw)
        stage[slot] = dot(xs, ggug[...].reshape(SIDE * SIDE * slots, 256), TN)
        for c in outs(j):
            c.start()
        return carry

    def down_step(j, carry):
        slot = lax.rem(j, 2)

        def out(i):
            return pltpu.make_async_copy(
                stage_d.at[slot], down_hbm.at[:, span(i, gw)], out_d_sem.at[slot]
            )

        @pl.when(j >= 2)
        def _():
            out(j - 2).wait()

        gs = rows[1, :, :, span(j, gw)].reshape(SIDE * SIDE * slots, gw)
        stage_d[slot] = dot(act[...].reshape(SIDE * SIDE * slots, 128), gs, TN)
        out(j).start()
        return carry

    n_g = width // gw
    lax.fori_loop(0, n_g, down_step, 0)
    for c in range(2):
        for a in range(2):
            near_after(a, c)
    lax.fori_loop(0, n_g, grad_step, 0)

    for c in range(2):
        for a in range(2):
            for k in (2, 3, 4, 5):
                rs[a][c][k].wait_recv()

            def put_part(v, s, a=a):
                t = v + rn[a, 0, :, :, s].astype(F32) + rn[a, 1, :, :, s].astype(F32)
                part[a, :, :, s] = t.astype(BF)

            terms(a, c, p_of[a], (0, 1, 2, 3), put_part)
            for k in (6, 7, 8, 9):
                rs[a][c][k].start()
    for c in range(2):
        ce = pl.ds(c * eighth, eighth)
        for a in range(2):
            for k, off, col0, r in ((6, 1, 0, 0), (7, 3, eighth, 1)):
                rs[a][c][k].wait_recv()
                b = ring(q_of[a], off)
                s = pl.ds(c * quarter + col0, eighth)
                t = part[a, b, :, s].astype(F32) + rf2[a, r, :, ce].astype(F32)
                part[a, b, :, s] = t.astype(BF)
                rs[a][c][k + 4].start()

    for c in y_copies[0]:
        c.wait_send()
    spread = jnp.where(
        (lax.broadcasted_iota(jnp.int32, (cols, slots), 1) // CAP) * PAD
        + lax.rem(lax.broadcasted_iota(jnp.int32, (cols, slots), 1), CAP)
        == lax.broadcasted_iota(jnp.int32, (cols, slots), 0),
        1.0,
        0.0,
    ).astype(BF)
    back_copies = []
    for c in range(2):
        for a in range(2):
            for k in (8, 9, 10, 11):
                rs[a][c][k].wait_recv()
            first_col = a * half + c * quarter

            def final_step(j, carry, a=a, c=c, first_col=first_col):
                s = part_span(c * quarter, j)
                t = part[a, q_of[a], :, s].astype(F32) + rn2[a, 0, :, s].astype(F32)
                t = (t + rn2[a, 1, :, s].astype(F32)).astype(BF)
                v = dot(spread, t, NN).astype(BF).reshape(n_out, PAD, eighth)
                ysend[0, :, :, part_span(first_col, j)] = v
                return carry

            lax.fori_loop(0, 2, final_step, 0)
            seg = pl.ds(first_col, quarter)
            for d in range(1, n_out):
                copy = pltpu.make_async_remote_copy(
                    src_ref=ysend.at[0, peer(d), :, seg],
                    dst_ref=back.at[me_o, :, seg],
                    send_sem=b_send_sem.at[a, c, d],
                    recv_sem=b_recv_sem.at[a, c, d],
                    device_id=(peer(d), me_i),
                    device_id_type=MESH,
                )
                copy.start()
                back_copies.append(copy)
            back[me_o, :, seg] = ysend[0, me_o, :, seg]
    back_outs = []
    for c in range(2):
        for a in range(2):
            seg = pl.ds(a * half + c * quarter, quarter)
            for d in range(1, n_out):
                pltpu.make_async_remote_copy(
                    src_ref=ysend.at[0, 0, :, seg],
                    dst_ref=back.at[lax.rem(me_o + n_out - d, n_out), :, seg],
                    send_sem=b_send_sem.at[a, c, d],
                    recv_sem=b_recv_sem.at[a, c, d],
                    device_id=(peer(d), me_i),
                    device_id_type=MESH,
                ).wait_recv()
            copy = pltpu.make_async_copy(
                back.at[:, :, seg], back_hbm.at[:, :, seg], b_out_sem.at[a, c]
            )
            copy.start()
            back_outs.append(copy)

    for c in started:
        c.wait_send()
    for c in y_copies[1]:
        c.wait_send()
    for c in back_copies:
        c.wait_send()
    for a in range(2):
        for chunk in rs[a]:
            for c in chunk:
                c.wait_send()
    for i in (n_g - 2, n_g - 1):
        slot = i % 2
        dst = pl.ds(i * gw, gw)
        pltpu.make_async_copy(
            stage.at[slot, :, pl.ds(0, 128)], gate_hbm.at[dst, :], out_sem.at[0, slot]
        ).wait()
        pltpu.make_async_copy(
            stage.at[slot, :, pl.ds(128, 128)], up_hbm.at[dst, :], out_sem.at[1, slot]
        ).wait()
        pltpu.make_async_copy(
            stage_d.at[slot], down_hbm.at[:, dst], out_d_sem.at[slot]
        ).wait()
    for c in back_outs:
        c.wait()
    place_out.wait()


def shards(layer_input, out_grad, expert_ids, route_scales, w_gate, w_up, w_down):
    toks, width = layer_input.shape
    n_out = lax.axis_size("outer")
    n_in = lax.axis_size("inner")
    hidden = w_gate.shape[2]
    slots = n_out * CAP
    half, quarter = width // 2, width // 4
    any_spec = pl.BlockSpec(memory_space=pl.ANY)
    vmem = pl.BlockSpec(memory_space=pltpu.VMEM)
    dma = pltpu.SemaphoreType.DMA
    back, place, gate, up, down = pl.pallas_call(
        kernel,
        out_shape=(
            jax.ShapeDtypeStruct((n_out, PAD, width), BF),
            jax.ShapeDtypeStruct((toks, n_out * PAD), BF),
            jax.ShapeDtypeStruct((width, hidden), F32),
            jax.ShapeDtypeStruct((width, hidden), F32),
            jax.ShapeDtypeStruct((hidden, width), F32),
        ),
        in_specs=[vmem, vmem] + [any_spec] * 5,
        out_specs=(any_spec,) * 5,
        scratch_shapes=[
            pltpu.VMEM((2, toks, width), BF),
            pltpu.VMEM((width, 2 * hidden), BF),
            pltpu.VMEM((hidden, width), BF),
            pltpu.VMEM((toks, n_out * PAD), BF),
            pltpu.VMEM((2, n_out, PAD, width), BF),
            pltpu.VMEM((2, n_out, PAD, width), BF),
            pltpu.VMEM((n_out, PAD, width), BF),
            pltpu.VMEM((2, n_in, slots, width), BF),
            pltpu.VMEM((n_in, slots, 2 * hidden), F32),
            pltpu.VMEM((n_in, slots, hidden), F32),
            pltpu.VMEM((n_in, slots, 2 * hidden), BF),
            pltpu.VMEM((n_in, slots, hidden), BF),
            pltpu.VMEM((2, 2, 2, slots, half), BF),
            pltpu.VMEM((2, 2, 2, slots, half), BF),
            pltpu.VMEM((2, 2, SIDE, slots, half), BF),
            pltpu.VMEM((2, 2, SIDE, slots, half), BF),
            pltpu.VMEM((2, SIDE, slots, half), BF),
            pltpu.VMEM((2, 2, slots, quarter), BF),
            pltpu.VMEM((2, 2, slots, half), BF),
            pltpu.VMEM((2, 512, 2 * hidden), F32),
            pltpu.VMEM((2, hidden, 512), F32),
            dma((5,)),
            dma((2, 2, n_out)),
            dma((2, 2, n_out)),
            dma((2, 2, n_out)),
            dma((2, 2, n_out)),
            dma((2, 20, 2)),
            dma((2, 20, 2)),
            dma((2, 2, 12)),
            dma((2, 2, 12)),
            dma((2, 2)),
            dma((2,)),
            dma((2, 2)),
            dma,
        ],
        compiler_params=pltpu.CompilerParams(
            collective_id=0, has_side_effects=True, vmem_limit_bytes=67043328
        ),
        name="expert_backward",
    )(expert_ids.T, route_scales.T, layer_input, out_grad, w_gate[0], w_up[0], w_down[0])
    in_grad = dot(place, back.reshape(n_out * PAD, width), NN).astype(BF)
    return in_grad, gate[None], up[None], down[None]


def solution(mesh):
    return jax.shard_map(
        shards,
        mesh=mesh,
        in_specs=(
            P(("outer", "inner"), None),
            P(("outer", "inner"), None),
            P(("outer", "inner"), None),
            P(("outer", "inner"), None),
            P("outer", None, "inner"),
            P("outer", None, "inner"),
            P("outer", "inner", None),
        ),
        out_specs=(
            P(("outer", "inner"), None),
            P("outer", None, "inner"),
            P("outer", None, "inner"),
            P("outer", "inner", None),
        ),
        check_vma=False,
    )
```
